32 devices in a mesh: sx: 8 (over y, x, core), sy: 4 (over z).
Axes of the slice: x: 2, y: 2, z: 4, core: 2. Of those that a mesh axis runs over, the one named last changes fastest.
Arguments:
- adjoint_loads: float32 [8, 8, 2, 288, 128], P('sx', 'sy'), may hold values from -6 to 6
- dual_taut: bfloat16 [8, 8, 1152, 1152], P('sx', 'sy'), may hold values from -1 to 2
- dual_wrinkle: bfloat16 [8, 8, 1152, 1152], P('sx', 'sy'), may hold values from -1 to 2
- dirichlet_taut: bfloat16 [8, 8, 1152, 1152], P('sx', 'sy'), may hold values from -1 to 2
- dirichlet_wrinkle: bfloat16 [8, 8, 1152, 1152], P('sx', 'sy'), may hold values from -1 to 2
- coupling: bfloat16 [8, 8, 12, 1152], P('sx', 'sy'), may hold values from -0.25 to 0.25
- coarse_inverse: bfloat16 [256, 256], P('sx', 'sy'), may hold values from -1 to 2
- wrinkled: int32 [8, 8], P('sx', 'sy'), may hold values 0 or 1
- edge_lengths: int32 [8, 8, 2], P('sx', 'sy'), may hold values from 144 to 288
- corner_map: int32 [8, 8, 12], P('sx', 'sy'), may hold values from 0 to 255, as said below
Outputs:
- multipliers: float32 [8, 8, 2, 288, 128], P('sx', 'sy')
- preconditioned: float32 [8, 8, 2, 288, 128], P('sx', 'sy')
The draws below stay inside these ranges and needn't reach their ends.
Inputs may be any that keep to these rules, and one draw needn't show every extreme that they name: `corner_map`: each subdomain names 12 distinct coarse indices, three for each of its four grid corners; subdomains that meet at a grid corner name the same three indices for it; distinct grid corners name distinct indices.
All inputs are finite; a program needn't handle non-finite values. No bound on the sum of `wrinkled` on one device may be relied on, other than what follows from the above.
Results may differ from the reference program's by a relative error of at most 0.012.
Values may be sent and summed in bfloat16 or wider, within the bound.
A program may use at most 64 MiB of HBM per device.

```python
import jax
import jax.numpy as jnp
from jax import lax

ORDER = 1152
EDGE = 288
LOADS = 128
CORNERS = 12
ITERS = 2
SUB_ROWS = 8
SUB_COLS = 8
COARSE = 256


def dominant(key, lead, size, low, high, spread_off):
    diag_key, off_key = jax.random.split(key)
    diagonal = jax.random.uniform(diag_key, lead + (size,), jnp.float32, low, high)
    off_part = jnp.clip(jax.random.normal(off_key, lead + (size, size), jnp.float32), -4.0, 4.0)
    off_part = off_part * (spread_off / size ** 0.5)
    return (off_part + jnp.eye(size, dtype=jnp.float32) * diagonal[..., None]).astype(jnp.bfloat16)


def draw_dual_taut(key, part):
    return dominant(jax.random.fold_in(key, 11), (SUB_ROWS, SUB_COLS), ORDER, 0.5, 1.5, 0.5)


def draw_dual_wrinkle(key, part):
    return dominant(jax.random.fold_in(key, 12), (SUB_ROWS, SUB_COLS), ORDER, 0.3, 0.9, 0.3)


def draw_dirichlet_taut(key, part):
    return dominant(jax.random.fold_in(key, 13), (SUB_ROWS, SUB_COLS), ORDER, 0.5, 1.5, 0.5)


def draw_dirichlet_wrinkle(key, part):
    return dominant(jax.random.fold_in(key, 14), (SUB_ROWS, SUB_COLS), ORDER, 0.3, 0.9, 0.3)


def draw_coarse_inverse(key, part):
    return dominant(jax.random.fold_in(key, 15), (), COARSE, 0.5, 1.5, 0.8)


def draw_corner_map(key, part):
    shuffled = jax.random.permutation(jax.random.fold_in(key, 21), COARSE)
    row_ids = jnp.arange(SUB_ROWS)[:, None, None]
    column_ids = jnp.arange(SUB_COLS)[None, :, None]
    slot_ids = jnp.arange(CORNERS)[None, None, :]
    corner_slot = slot_ids // 3
    down_step = jnp.array([0, 0, 1, 1])[corner_slot]
    right_step = jnp.array([0, 1, 1, 0])[corner_slot]
    grid_point = (row_ids + down_step) * (SUB_COLS + 1) + column_ids + right_step
    return shuffled[3 * grid_point + slot_ids % 3].astype(jnp.int32)


def with_ends(drawn, own_key, smallest, largest):
    extent = drawn.shape
    place = [jax.random.randint(jax.random.fold_in(own_key, axis), (), 0, extent[axis]) for axis in range(len(extent))]
    drawn = drawn.at[tuple(place)].set(smallest)
    longest = extent.index(max(extent))
    place[longest] = (place[longest] + 1) % extent[longest]
    return drawn.at[tuple(place)].set(largest)


def steps_of(key, shape, pieces, smallest, high):
    def one(dim, blocks):
        heights = jax.random.uniform(jax.random.fold_in(jax.random.fold_in(key, 6), dim), (blocks,), jnp.float32, smallest / len(pieces), high / len(pieces))
        return jnp.repeat(jnp.exp(heights), shape[dim] // blocks).reshape((-1,) + (1,) * (len(shape) - dim - 1))

    level = one(*pieces[0])
    for cut in pieces[1:]:
        level = level * one(*cut)
    return level


def normal_values(own_key, shape, deviation, bound, cuts=(), held_as=jnp.bfloat16):
    values = jax.random.normal(own_key, shape, jnp.float32) * deviation
    if len(cuts) > 0:
        values = steps_of(own_key, shape, cuts, -0.22, 0.18) * values
    return jnp.clip(values, min=-bound, max=bound).astype(held_as)


def setup_inputs(seed: int = 0) -> dict:
    key_list = jax.random.split(jax.random.key(seed), 11)
    adjoint_loads = normal_values(key_list[0], (SUB_ROWS, SUB_COLS, 2, EDGE, LOADS), 1.0, 6.0, ((0, 8), (1, 4)), jnp.float32)
    dual_taut = draw_dual_taut(jax.random.fold_in(key_list[10], 71), 0)
    dual_wrinkle = draw_dual_wrinkle(jax.random.fold_in(key_list[10], 71), 0)
    dirichlet_taut = draw_dirichlet_taut(jax.random.fold_in(key_list[10], 71), 0)
    dirichlet_wrinkle = draw_dirichlet_wrinkle(jax.random.fold_in(key_list[10], 71), 0)
    coupling = normal_values(key_list[5], (SUB_ROWS, SUB_COLS, CORNERS, ORDER), (ORDER // 2) ** -0.5, 0.25, ((0, 8), (1, 4)))
    coarse_inverse = draw_coarse_inverse(jax.random.fold_in(key_list[10], 71), 0)
    wrinkled = with_ends((jax.random.randint(key_list[7], (SUB_ROWS, SUB_COLS), 0, 3) < 1).astype(jnp.int32), jax.random.fold_in(key_list[7], 1), 0, 1)
    edge_lengths = with_ends(jax.random.randint(key_list[8], (SUB_ROWS, SUB_COLS, 2), EDGE // 2, EDGE + 1), jax.random.fold_in(key_list[8], 1), EDGE // 2, EDGE).astype(jnp.int32)
    corner_map = draw_corner_map(jax.random.fold_in(key_list[10], 71), 0)
    return {"adjoint_loads": adjoint_loads, "dual_taut": dual_taut, "dual_wrinkle": dual_wrinkle, "dirichlet_taut": dirichlet_taut, "dirichlet_wrinkle": dirichlet_wrinkle, "coupling": coupling, "coarse_inverse": coarse_inverse, "wrinkled": wrinkled, "edge_lengths": edge_lengths, "corner_map": corner_map}


step_sizes = (0.55, 0.75)
momenta = (0.0, 0.15)


def edge_mask(edge_lengths):
    positions = jnp.arange(EDGE, dtype=jnp.int32)
    inside = positions[None, None, None, :] < edge_lengths[:, :, :, None]
    row_ids = jnp.arange(SUB_ROWS, dtype=jnp.int32)[:, None] + jnp.zeros((1, SUB_COLS), jnp.int32)
    column_ids = jnp.arange(SUB_COLS, dtype=jnp.int32)[None, :] + jnp.zeros((SUB_ROWS, 1), jnp.int32)
    exists = jnp.stack([column_ids < SUB_COLS - 1, row_ids < SUB_ROWS - 1], axis=2)
    return (inside & exists[:, :, :, None]).astype(jnp.float32)[..., None]


def spread(edges):
    east_edge = edges[:, :, 0]
    south_edge = edges[:, :, 1]
    west_edge = jnp.concatenate([jnp.zeros_like(east_edge[:, :1]), east_edge[:, :-1]], axis=1)
    north_edge = jnp.concatenate([jnp.zeros_like(south_edge[:1]), south_edge[:-1]], axis=0)
    return jnp.concatenate([east_edge, south_edge, -west_edge, -north_edge], axis=2)


def collect(local_part):
    west_part = local_part[:, :, 2 * EDGE:3 * EDGE]
    right_west = jnp.concatenate([west_part[:, 1:], jnp.zeros_like(west_part[:, :1])], axis=1)
    north_part = local_part[:, :, 3 * EDGE:]
    down_north = jnp.concatenate([north_part[1:], jnp.zeros_like(north_part[:1])], axis=0)
    return jnp.stack([local_part[:, :, :EDGE] - right_west, local_part[:, :, EDGE:2 * EDGE] - down_north], axis=2)


def paired(taut, wrinkle, wrinkled, vectors):
    def one_row(operands):
        taut_row, wrinkle_row, flag_row, vector_row = operands
        vector_wide = vector_row.astype(jnp.float32)
        base_part = jnp.einsum("sij,sjl->sil", taut_row.astype(jnp.float32), vector_wide)
        extra_part = jnp.einsum("sij,sjl->sil", wrinkle_row.astype(jnp.float32), vector_wide)
        return base_part + flag_row.astype(jnp.float32)[:, None, None] * extra_part

    return lax.map(one_row, (taut, wrinkle, wrinkled, vectors))


def coarse_term(coupling, corner_map, coarse_inverse, vectors):
    coupling_wide = coupling.astype(jnp.float32)
    corner_terms = jnp.einsum("rskj,rsjl->rskl", coupling_wide, vectors.astype(jnp.float32))
    corner_index = corner_map.reshape(-1).astype(jnp.int32)
    gathered = jnp.zeros((COARSE, LOADS), jnp.float32).at[corner_index].add(corner_terms.reshape(-1, LOADS))
    solved = jnp.dot(coarse_inverse, gathered.astype(jnp.bfloat16), preferred_element_type=jnp.float32).astype(jnp.bfloat16)
    selected = solved[corner_index].reshape(SUB_ROWS, SUB_COLS, CORNERS, LOADS)
    return jnp.einsum("rskj,rskl->rsjl", coupling_wide, selected.astype(jnp.float32))


def reference(adjoint_loads, dual_taut, dual_wrinkle, dirichlet_taut, dirichlet_wrinkle, coupling, coarse_inverse, wrinkled, edge_lengths, corner_map):
    masking = edge_mask(edge_lengths)
    loads = adjoint_loads * masking

    def dual_apply(incoming):
        vectors = spread(incoming.astype(jnp.bfloat16))
        local_part = paired(dual_taut, dual_wrinkle, wrinkled, vectors)
        local_part = local_part + coarse_term(coupling, corner_map, coarse_inverse, vectors)
        return collect(local_part) * masking

    def precondition(incoming):
        vectors = spread((0.5 * incoming).astype(jnp.bfloat16))
        return 0.5 * collect(paired(dirichlet_taut, dirichlet_wrinkle, wrinkled, vectors)) * masking

    multipliers = jnp.zeros_like(loads)
    direction = jnp.zeros_like(loads)
    residual = loads
    for number in range(ITERS):
        direction = precondition(residual) + momenta[number] * direction
        multipliers = multipliers + step_sizes[number] * direction
        residual = loads - dual_apply(multipliers)
    return multipliers, precondition(residual)
```

```python
import functools

import jax
import jax.numpy as jnp
from jax import lax
from jax.experimental import pallas as pl
from jax.experimental.pallas import tpu as pltpu
from jax.sharding import PartitionSpec as P

ITERS = 2
step_sizes = (0.55, 0.75)
momenta = (0.0, 0.15)

MESH = pl.DeviceIdType.MESH
SLOT = 16
LANES = 128
F32 = jnp.float32
BF16 = jnp.bfloat16
EAST, SOUTH, WEST, NORTH = 0, 1, 2, 3


def sizes_of(nr, ns, per, corners, tr, tc):
    listed = -(-(3 * per + 2) * SLOT // LANES) * LANES
    distinct = -(-(corners // 4) * (4 * per + 8) // SLOT) * SLOT
    pack = 2 if 2 * tc <= LANES and tr % (2 * SLOT) == 0 else 1
    lanes = -(-pack * tc // LANES) * LANES
    return listed, distinct, pack, tr // pack, lanes


def kernel(
    nr, ns,
    loads_in, dual_t, dual_w, diri_t, diri_w, coup_in, cinv_in, wr_in, len_in, cm_in,
    mult_out, prec_out,
    am, aw, bm, bw, vec, loc, snd, rcv, ld, mu, di,
    lraw, craw, vraw, wr_ref, len_ref, cm_ref,
    meta, nmeta, lens, jcol, dmat, dtm, ub, ux, uz, kp, kmat,
    cedge, cnbr, ce, cet, corr, tdir, tsum, ts, tp, ys, yr,
    mat_sem, in_sem, h_send, h_recv, m_send, m_recv, c_send, c_recv,
    ux_send, ux_recv, uz_send, uz_recv, k1_send, k1_recv, k2_send, k2_recv, k3_send, k3_recv,
    t_send, t_recv, y_send, y_recv,
):
    r, s = lax.axis_index("sx"), lax.axis_index("sy")
    per = loads_in.shape[1]
    edge, width = loads_in.shape[3], loads_in.shape[4]
    corners = coup_in.shape[1]
    tr, tc = cinv_in.shape
    listed, distinct, pack, tp_rows, kl = sizes_of(nr, ns, per, corners, tr, tc)
    rows = per * SLOT
    half = nr // 2
    odd = lax.rem(r, 2)
    has_left, has_right = s > 0, s < ns - 1
    has_up, has_down = r > 0, r < nr - 1
    exists = {EAST: has_right, SOUTH: has_down, WEST: has_left, NORTH: has_up}
    far, near = 3 - 2 * odd, 1 + 2 * odd
    has_far = ((odd == 1) & has_down) | ((odd == 0) & has_up)
    has_near = ((odd == 0) & has_down) | ((odd == 1) & has_up)

    barrier = pltpu.get_barrier_semaphore()
    for k in range(1, nr):
        pl.semaphore_signal(barrier, inc=1, device_id={"sx": lax.rem(r + k, nr)}, device_id_type=MESH)
    for k in range(1, ns):
        pl.semaphore_signal(barrier, inc=1, device_id={"sy": lax.rem(s + k, ns)}, device_id_type=MESH)

    small = [
        pltpu.make_async_copy(src, dst, in_sem.at[i])
        for i, (src, dst) in enumerate(
            ((wr_in, wr_ref), (len_in, len_ref), (cm_in, cm_ref), (loads_in.at[0], lraw), (coup_in.at[0], craw), (cinv_in, vraw))
        )
    ]
    for copy in small:
        copy.start()
    mats_in = []
    for i, (src, dst) in enumerate(((diri_t, am), (diri_w, aw), (dual_t, bm), (dual_w, bw))):
        for c in range(per):
            mats_in.append(pltpu.make_async_copy(src.at[0, c], dst.at[c], mat_sem.at[i * per + c]))
    for c in range(per):
        for i in (0, 1):
            mats_in[i * per + c].start()

    positions = lax.broadcasted_iota(jnp.int32, (edge, width), 0)

    def live(row):
        return positions < jnp.broadcast_to(row, (edge, width))

    def mask_of(i):
        return live(lens[pl.ds(i, 1), :])

    def rows_of(e):
        return pl.ds(pl.multiple_of(e * edge, SLOT), edge)

    def put(c, e, value):
        vec[c, rows_of(e)] = value.astype(BF16)

    def xfer(k, c, e, axis):
        if axis == "sy":
            to, land = s + (1 - e), (0 if e == EAST else per - 1) * 4 + 2 - e
        else:
            to, land = r + (2 - e), c * 4 + 4 - e
        return pltpu.make_async_remote_copy(
            src_ref=snd.at[k, c * 4 + e], dst_ref=rcv.at[k, land],
            send_sem=h_send.at[k, c * 4 + e], recv_sem=h_recv.at[k, land],
            device_id={axis: to}, device_id_type=MESH,
        )

    def landed(k, c, e):
        return pltpu.make_async_remote_copy(
            src_ref=snd.at[k, c * 4 + e], dst_ref=rcv.at[k, c * 4 + e],
            send_sem=h_send.at[k, c * 4 + e], recv_sem=h_recv.at[k, c * 4 + e],
            device_id={"sx": r}, device_id_type=MESH,
        )

    def ship(k, what, there, axis):
        @pl.when(there)
        def _():
            for c, e in what:
                xfer(k, c, e, axis).start()

    def arrive(k, what, there):
        @pl.when(there)
        def _():
            for c, e in what:
                landed(k, c, e).wait_recv()

    def outer():
        return [(0, WEST, has_left, "sy"), (per - 1, EAST, has_right, "sy")]

    def peer_copy(axis, k, src, dst, ssem, rsem):
        n, me = (nr, r) if axis == "sx" else (ns, s)
        return pltpu.make_async_remote_copy(
            src_ref=src, dst_ref=dst, send_sem=ssem.at[k], recv_sem=rsem.at[k],
            device_id={axis: lax.rem(me + k, n)}, device_id_type=MESH,
        )

    def meta_copy(e):
        axis, to = ("sy", s + (1 - e)) if e in (EAST, WEST) else ("sx", r + (2 - e))
        land = (2 - e) if e in (EAST, WEST) else (4 - e)
        return pltpu.make_async_remote_copy(
            src_ref=meta, dst_ref=nmeta.at[land], send_sem=m_send.at[e], recv_sem=m_recv.at[land],
            device_id={axis: to}, device_id_type=MESH,
        )

    def coupling_copy(c, e):
        axis, to = ("sy", s + (1 - e)) if e in (EAST, WEST) else ("sx", r + (2 - e))
        land = (0 if e == EAST else per - 1) * 4 + 2 - e if e in (EAST, WEST) else c * 4 + 4 - e
        return pltpu.make_async_remote_copy(
            src_ref=cedge.at[c * 4 + e], dst_ref=cnbr.at[land], send_sem=c_send.at[c * 4 + e], recv_sem=c_recv.at[land],
            device_id={axis: to}, device_id_type=MESH,
        )

    shared = [(c, SOUTH) for c in range(per)] + [(c, NORTH) for c in range(per)] + [(per - 1, EAST), (0, WEST)]

    for copy in small[:3]:
        copy.wait()
    meta[...] = jnp.full(meta.shape, -1, jnp.int32)
    for c in range(per):
        for m in range(corners):
            meta[c * SLOT + m : c * SLOT + m + 1, :] = jnp.full((1, LANES), cm_ref[0, c, m], jnp.int32)
        east = len_ref[0, c, 0]
        if c == per - 1:
            east = jnp.where(has_right, east, 0)
        south = jnp.where(has_down, len_ref[0, c, 1], 0)
        for e, length in ((EAST, east), (SOUTH, south)):
            row = jnp.full((1, LANES), length, jnp.int32)
            meta[rows + 2 * c + e : rows + 2 * c + e + 1, :] = row
            lens[c * 4 + e : c * 4 + e + 1, :] = row
    small[3].wait()
    for c in range(per):
        for e in (EAST, SOUTH):
            value = jnp.where(live(lens[c * 4 + e : c * 4 + e + 1, :]), lraw[c, e], 0.0)
            ld[c * 4 + e] = value
            put(c, e, 0.5 * value)
            if e == SOUTH or c == per - 1:
                snd[0, c * 4 + e] = value.astype(BF16)
            else:
                put(c + 1, WEST, -0.5 * value)
    small[4].wait()
    small[5].wait()
    for c in range(per):
        whole = jnp.concatenate(
            [craw[:, c, :].astype(F32), jnp.zeros((SLOT - corners, craw.shape[2]), F32)], axis=0
        )
        turned = whole.T
        for e in range(4):
            cedge[c * 4 + e] = turned[e * edge : (e + 1) * edge].T.astype(BF16)
    tile = vraw[...].astype(F32)
    parts = [tile[h * tp_rows : (h + 1) * tp_rows] for h in range(pack)]
    if kl > pack * tc:
        parts.append(jnp.zeros((tp_rows, kl - pack * tc), F32))
    kp[odd, lax.div(r, 2), s] = jnp.concatenate(parts, axis=1).astype(BF16)

    pl.semaphore_wait(barrier, nr - 1 + ns - 1)
    ship(0, [(c, SOUTH) for c in range(per)], has_down, "sx")
    ship(0, [(per - 1, EAST)], has_right, "sy")
    for e in range(4):
        @pl.when(exists[e])
        def _(e=e):
            meta_copy(e).start()
            for c, f in shared:
                if f == e:
                    coupling_copy(c, e).start()
    mine = kp.at[odd, lax.div(r, 2)]
    k1 = [peer_copy("sy", k, mine.at[s], mine.at[s], k1_send, k1_recv) for k in range(1, ns)]
    k2 = [
        pltpu.make_async_remote_copy(
            src_ref=mine, dst_ref=mine, send_sem=k2_send.at[k], recv_sem=k2_recv.at[k],
            device_id={"sx": lax.rem(r + 2 * k, nr)}, device_id_type=MESH,
        )
        for k in range(1, half)
    ]
    k3 = pltpu.make_async_remote_copy(
        src_ref=kp.at[odd], dst_ref=kp.at[odd], send_sem=k3_send.at[0], recv_sem=k3_recv.at[0],
        device_id={"sx": r + 1 - 2 * odd}, device_id_type=MESH,
    )
    for copy in k1:
        copy.start()

    def combine(c, main, extra):
        flag = jnp.full((1, 1), wr_ref[0, c], jnp.int32).astype(F32).astype(BF16)
        size = main.shape[1]
        step = 128

        def body(i, _):
            part = pl.ds(pl.multiple_of(i * step, step), step)
            main[c, part] = main[c, part] + flag * extra[c, part]
            return 0

        lax.fori_loop(0, size // step, body, 0)

    for c in range(per):
        mats_in[c].wait()
        mats_in[per + c].wait()
        mats_in[2 * per + c].start()
        mats_in[3 * per + c].start()
        combine(c, am, aw)

    for e in range(4):
        @pl.when(exists[e])
        def _(e=e):
            meta_copy((2 - e) if e in (EAST, WEST) else (4 - e)).wait_recv()
    for copy in k1:
        copy.wait_recv()
    for copy in k2:
        copy.start()
    for c in range(per):
        row = nmeta[NORTH, rows + 2 * c + SOUTH : rows + 2 * c + SOUTH + 1, :]
        lens[c * 4 + NORTH : c * 4 + NORTH + 1, :] = jnp.where(has_up, row, 0)
    row = nmeta[WEST, rows + 2 * (per - 1) + EAST : rows + 2 * (per - 1) + EAST + 1, :]
    lens[WEST : WEST + 1, :] = jnp.where(has_left, row, 0)

    place = {}
    jcol[...] = jnp.full(jcol.shape, -1, jnp.int32)
    for c in range(per):
        jcol[c * SLOT : (c + 1) * SLOT, :] = meta[c * SLOT : (c + 1) * SLOT, :]
    for i, (c, e) in enumerate(shared):
        place[c, e] = (per + i) * SLOT
        theirs = (0 if e == EAST else per - 1 if e == WEST else c) * SLOT
        jcol[place[c, e] : place[c, e] + SLOT, :] = jnp.where(exists[e], nmeta[e, theirs : theirs + SLOT, :], -1)
    for c in range(per - 1):
        place[c, EAST] = (c + 1) * SLOT
    square = (listed, listed)
    jf = jnp.broadcast_to(jcol[:, 0:1], square).astype(F32)
    jr = jf.T
    row_id = lax.broadcasted_iota(jnp.int32, square, 0)
    lane_id = lax.broadcasted_iota(jnp.int32, square, 1)
    again = jnp.max(jnp.where((jf == jr) & (lane_id < row_id), 1.0, 0.0), axis=1, keepdims=True)
    first = jnp.where(jf[:, 0:1] >= 0.0, 1.0 - again, 0.0)
    first_row = jnp.broadcast_to(first, square).T
    rank = jnp.sum(jnp.where(lane_id < row_id, first_row, 0.0), axis=1, keepdims=True)
    chosen = (jnp.broadcast_to(rank, square) == lane_id.astype(F32)) & (jnp.broadcast_to(first, square) > 0.5)
    u_row = jnp.sum(jnp.where(chosen, jf + 1.0, 0.0), axis=0, keepdims=True) - 1.0
    u_lanes = jnp.broadcast_to(u_row, square)
    u_rows = u_lanes.T
    dmat[...] = jnp.where((u_rows == jr) & (jr >= 0.0), 1.0, 0.0)[0:distinct].astype(BF16)
    dtm[...] = jnp.where((jf == u_lanes) & (jf >= 0.0), 1.0, 0.0)[:, 0:distinct].astype(BF16)
    u_block = jnp.broadcast_to(u_row, ub.shape).astype(jnp.int32)
    ub[...] = u_block
    ux[pl.ds(r, 1)] = u_block[None]
    uz[pl.ds(s, 1)] = u_block[None]
    uxc = [peer_copy("sx", k, ub, ux.at[r], ux_send, ux_recv) for k in range(1, nr)]
    uzc = [peer_copy("sy", k, ub, uz.at[s], uz_send, uz_recv) for k in range(1, ns)]
    for copy in uxc + uzc:
        copy.start()

    for c in range(per):
        for e in range(4):
            if (c, e) not in place:
                continue
            if (c, e) in shared:
                @pl.when(exists[e])
                def _(c=c, e=e):
                    pltpu.make_async_remote_copy(
                        src_ref=cedge.at[c * 4 + e], dst_ref=cnbr.at[c * 4 + e],
                        send_sem=c_send.at[c * 4 + e], recv_sem=c_recv.at[c * 4 + e],
                        device_id={"sx": r}, device_id_type=MESH,
                    ).wait_recv()
                theirs = jnp.where(exists[e], cnbr[c * 4 + e].astype(F32), 0.0)
            else:
                theirs = cedge[(c + 1) * 4 + WEST].astype(F32)
            both = jnp.concatenate([cedge[c * 4 + e].astype(F32), -theirs], axis=0)
            ce[c * 4 + e] = both.astype(BF16)

    def setup_turned():
        for c, e in place:
            cet[c * 4 + e] = ce[c * 4 + e].astype(F32).T.astype(BF16)

    def setup_coarse():
        for copy in uxc + uzc:
            copy.wait_recv()
        k3.wait_recv()
        count = ns * distinct
        wanted = jnp.concatenate(
            [jnp.broadcast_to(uz[q, 0:1, :].astype(F32), square).T[0:distinct, 0:1] for q in range(ns)], axis=0
        )
        at = lax.broadcasted_iota(jnp.int32, (8, nr * tp_rows), 1)
        index = at
        start = [(2 * (m % half) + m // half) * tr for m in range(nr)]
        for m in range(1, nr):
            jump = (start[m] - m * tp_rows) - (start[m - 1] - (m - 1) * tp_rows)
            index = index + jnp.where(at >= m * tp_rows, jump, 0)
        index = index.astype(F32)[0:1]
        lane = lax.broadcasted_iota(jnp.int32, (count, kl), 1)
        picks = [
            jnp.where(
                jnp.broadcast_to(wanted, (count, nr * tp_rows)) == jnp.broadcast_to(index + h * tp_rows, (count, nr * tp_rows)),
                1.0, 0.0,
            ).astype(BF16)
            for h in range(pack)
        ]
        chosen_rows = []
        for q in range(ns):
            plane = kp[:, :, q].astype(F32).reshape(nr * tp_rows, kl).astype(BF16)
            total = jnp.zeros((count, kl), F32)
            for h in range(pack):
                found = jnp.dot(picks[h], plane, preferred_element_type=F32)
                total = jnp.where((lane >= h * tc) & (lane < (h + 1) * tc), found, total)
            chosen_rows.append(total.astype(BF16))
        chosen_rows = jnp.concatenate(chosen_rows, axis=1)
        deep = lax.broadcasted_iota(jnp.int32, (ns * kl, listed), 0)
        column = jnp.full((ns * kl, listed), -5, jnp.int32)
        for q in range(ns):
            for h in range(pack):
                low = q * kl + h * tc
                column = jnp.where((deep >= low) & (deep < low + tc), deep - low + q * tc, column)
        for q in range(nr):
            pick = jnp.where(column == jnp.broadcast_to(ux[q, 0:1, :], column.shape), 1.0, 0.0).astype(BF16)
            kmat[q] = jnp.dot(chosen_rows, pick, preferred_element_type=F32)[:, 0:distinct].astype(BF16)

    def products(k, mat, what):
        for c, e in what:
            value = jnp.dot(mat[c, rows_of(e), :], vec[c], preferred_element_type=F32)
            loc[c, rows_of(e)] = value
            if k is not None:
                snd[k, c * 4 + e] = value.astype(BF16)

    def own(c, e):
        return loc[c, rows_of(e)]

    far_edges = [(c, far) for c in range(per)]
    near_edges = [(c, near) for c in range(per)]
    inner_blocks = [(c, EAST) for c in range(per - 1)] + [(c, WEST) for c in range(1, per)]

    def apply(k, mat):
        products(k, mat, far_edges)
        ship(k, far_edges, has_far, "sx")
        products(k, mat, [(0, WEST), (per - 1, EAST)])
        for c, e, there, axis in outer():
            ship(k, [(c, e)], there, axis)
        products(k, mat, near_edges)
        ship(k, near_edges, has_near, "sx")
        products(None, mat, inner_blocks)

    def gathered(k, c, e):
        return own(c, e) - rcv[k, c * 4 + e].astype(F32)

    def exchanged(k, act):
        for c in range(per - 1):
            act(c, EAST, own(c, EAST) - own(c + 1, WEST))
        arrive(k, near_edges, has_near)
        for c, e in near_edges:
            act(c, e, gathered(k, c, e))
        for c, e, there, _ in outer():
            arrive(k, [(c, e)], there)
            act(c, e, gathered(k, c, e))
        arrive(k, far_edges, has_far)
        for c, e in far_edges:
            act(c, e, gathered(k, c, e))

    def is_inner(c, e):
        return isinstance(e, int) and e == EAST and c < per - 1

    arrive(0, [(0, WEST)], has_left)
    value = jnp.where(jnp.broadcast_to(has_left, (edge, width)), -rcv[0, WEST].astype(F32), 0.0)
    ld[WEST] = value
    put(0, WEST, 0.5 * value)
    arrive(0, [(c, NORTH) for c in range(per)], has_up)
    for c in range(per):
        value = jnp.where(jnp.broadcast_to(has_up, (edge, width)), -rcv[0, c * 4 + NORTH].astype(F32), 0.0)
        ld[c * 4 + NORTH] = value
        put(c, NORTH, 0.5 * value)

    halo_round = 1
    for number in range(ITERS):
        apply(halo_round, am)

        acc = [jnp.zeros((SLOT, width), F32) for _ in range(listed // SLOT)]
        for (c, e), at in place.items():
            if is_inner(c, e):
                value = own(c, e) - own(c + 1, WEST)
            else:
                value = snd[halo_round, c * 4 + e].astype(F32)
            value = jnp.where(mask_of(c * 4 + e), value, 0.0).astype(BF16)
            both = jnp.dot(ce[c * 4 + e], value, preferred_element_type=F32)
            acc[c] = acc[c] + both[0:SLOT]
            acc[at // SLOT] = acc[at // SLOT] + both[SLOT:]
        terms = 0.5 * jnp.concatenate(acc, axis=0)
        high = terms.astype(BF16)
        low = (terms - high.astype(F32)).astype(BF16)
        terms = jnp.dot(dmat[...], high, preferred_element_type=F32) + jnp.dot(dmat[...], low, preferred_element_type=F32)
        if number > 0:
            terms = terms + momenta[number] * tdir[...]
        tdir[...] = terms
        terms = step_sizes[number] * terms
        if number > 0:
            terms = terms + tsum[...]
        tsum[...] = terms
        terms = terms.astype(BF16)
        ts[number] = terms
        tp[number, pl.ds(r, 1)] = terms[None]
        tcopies = [
            peer_copy("sx", k, ts.at[number], tp.at[number, r], t_send.at[number], t_recv.at[number])
            for k in range(1, nr)
        ]
        for copy in tcopies:
            copy.start()

        if number == 0:
            for copy in k2:
                copy.wait_recv()
            k3.start()
            for c in range(per):
                mats_in[2 * per + c].wait()
                mats_in[3 * per + c].wait()
                combine(c, bm, bw)
            setup_turned()
            setup_coarse()

        def advance(c, e, value):
            i = c * 4 + e
            value = jnp.where(mask_of(i), 0.5 * value, 0.0)
            if number == 0:
                iterate = step_sizes[0] * value
            else:
                value = value + momenta[number] * di[i]
                iterate = mu[i] + step_sizes[number] * value
            if number < ITERS - 1:
                di[i] = value
            mu[i] = iterate
            put(c, e, iterate)
            if is_inner(c, e):
                put(c + 1, WEST, -iterate)

        exchanged(halo_round, advance)
        halo_round += 1

        apply(halo_round, bm)
        for copy in tcopies:
            copy.wait_recv()
        partial = jnp.dot(kmat[0], tp[number, 0], preferred_element_type=F32)
        for q in range(1, nr):
            partial = partial + jnp.dot(kmat[q], tp[number, q], preferred_element_type=F32)
        ys[number] = partial.astype(BF16).reshape(ns, distinct, width)
        yr[number, pl.ds(s, 1)] = ys[number, pl.ds(s, 1)]
        ycopies = [
            peer_copy(
                "sy", k, ys.at[number, lax.rem(s + k, ns)], yr.at[number, s],
                y_send.at[number], y_recv.at[number],
            )
            for k in range(1, ns)
        ]
        for copy in ycopies:
            copy.start()
        if number == ITERS - 1:
            for c in range(per):
                for e in (EAST, SOUTH):
                    mult_out[0, c, e] = mu[c * 4 + e]
        for copy in ycopies:
            copy.wait_recv()
        solved = yr[number, 0].astype(F32)
        for q in range(1, ns):
            solved = solved + yr[number, q].astype(F32)
        solved = jnp.dot(dtm[...], solved.astype(BF16), preferred_element_type=F32)
        for (c, e), at in place.items():
            both = jnp.concatenate([solved[c * SLOT : (c + 1) * SLOT], solved[at : at + SLOT]], axis=0).astype(BF16)
            corr[c * 4 + e] = jnp.dot(cet[c * 4 + e], both, preferred_element_type=F32)

        def remain(c, e, value):
            i = c * 4 + e
            value = 0.5 * (ld[i] - jnp.where(mask_of(i), value + corr[i], 0.0))
            put(c, e, value)
            if is_inner(c, e):
                put(c + 1, WEST, -value)

        exchanged(halo_round, remain)
        halo_round += 1

    norths = [(c, NORTH) for c in range(per)]
    products(halo_round, am, norths)
    ship(halo_round, norths, has_up, "sx")
    products(halo_round, am, [(0, WEST)])
    ship(halo_round, [(0, WEST)], has_left, "sy")
    products(None, am, [(c, e) for c in range(per) for e in (EAST, SOUTH)] + [(c, WEST) for c in range(1, per)])

    def finish(c, e, value):
        prec_out[0, c, e] = jnp.where(mask_of(c * 4 + e), 0.5 * value, 0.0)

    for c in range(per - 1):
        finish(c, EAST, own(c, EAST) - own(c + 1, WEST))
    arrive(halo_round, [(per - 1, EAST)], has_right)
    finish(per - 1, EAST, gathered(halo_round, per - 1, EAST))
    arrive(halo_round, [(c, SOUTH) for c in range(per)], has_down)
    for c in range(per):
        finish(c, SOUTH, gathered(halo_round, c, SOUTH))

    for e in range(4):
        @pl.when(exists[e])
        def _(e=e):
            axis = "sy" if e in (EAST, WEST) else "sx"
            meta_copy(e).wait_send()
            for c, f in shared:
                if f == e:
                    coupling_copy(c, e).wait_send()
                    for k in range(halo_round + 1):
                        if not (k == 0 and e in (WEST, NORTH)) and not (k == halo_round and e in (EAST, SOUTH)):
                            xfer(k, c, e, axis).wait_send()
    for copy in k1 + k2 + [k3] + uxc + uzc:
        copy.wait_send()
    for number in range(ITERS):
        for k in range(1, nr):
            peer_copy("sx", k, ts.at[number], tp.at[number, r], t_send.at[number], t_recv.at[number]).wait_send()
        for k in range(1, ns):
            peer_copy(
                "sy", k, ys.at[number, lax.rem(s + k, ns)], yr.at[number, s], y_send.at[number], y_recv.at[number]
            ).wait_send()


def hand_over(mult_in, prec_in, mult_out, prec_out, sem):
    copies = [
        pltpu.make_async_copy(mult_in, mult_out, sem.at[0]),
        pltpu.make_async_copy(prec_in, prec_out, sem.at[1]),
    ]
    for copy in copies:
        copy.start()
    for copy in copies:
        copy.wait()


def local(nr, ns, *args):
    adjoint_loads, dual_taut, coupling, coarse_inverse = args[0], args[1], args[5], args[6]
    per, edge, width = adjoint_loads.shape[1], adjoint_loads.shape[3], adjoint_loads.shape[4]
    size = dual_taut.shape[-1]
    corners = coupling.shape[2]
    tr, tc = coarse_inverse.shape
    listed, distinct, pack, tp_rows, kl = sizes_of(nr, ns, per, corners, tr, tc)
    rows = per * SLOT
    rounds = 2 * ITERS + 2
    edges = 4 * per
    meta_rows = rows + -(-2 * per // 8) * 8
    dma = pltpu.SemaphoreType.DMA
    vmem = pl.BlockSpec(memory_space=pltpu.VMEM)
    hbm = pl.BlockSpec(memory_space=pl.ANY)
    args = args[:5] + (jnp.transpose(coupling, (0, 2, 1, 3)),) + args[6:]
    i32 = jnp.int32
    scratch = [pltpu.VMEM((per, size, size), BF16)] * 4 + [
        pltpu.VMEM((per, size, width), BF16),
        pltpu.VMEM((per, size, width), F32),
        pltpu.VMEM((rounds, edges, edge, width), BF16),
        pltpu.VMEM((rounds, edges, edge, width), BF16),
        pltpu.VMEM((edges, edge, width), F32),
        pltpu.VMEM((edges, edge, width), F32),
        pltpu.VMEM((edges, edge, width), F32),
        pltpu.VMEM(adjoint_loads.shape[1:], F32),
        pltpu.VMEM(args[5].shape[1:], BF16),
        pltpu.VMEM((tr, tc), BF16),
        pltpu.SMEM(args[7].shape, i32),
        pltpu.SMEM(args[8].shape, i32),
        pltpu.SMEM(args[9].shape, i32),
        pltpu.VMEM((meta_rows, LANES), i32),
        pltpu.VMEM((4, meta_rows, LANES), i32),
        pltpu.VMEM((-(-edges // 8) * 8, LANES), i32),
        pltpu.VMEM((listed, LANES), i32),
        pltpu.VMEM((distinct, listed), BF16),
        pltpu.VMEM((listed, distinct), BF16),
        pltpu.VMEM((8, listed), i32),
        pltpu.VMEM((nr, 8, listed), i32),
        pltpu.VMEM((ns, 8, listed), i32),
        pltpu.VMEM((2, nr // 2, ns, tp_rows, kl), BF16),
        pltpu.VMEM((nr, ns * distinct, distinct), BF16),
        pltpu.VMEM((edges, SLOT, edge), BF16),
        pltpu.VMEM((edges, SLOT, edge), BF16),
        pltpu.VMEM((edges, 2 * SLOT, edge), BF16),
        pltpu.VMEM((edges, edge, 2 * SLOT), BF16),
        pltpu.VMEM((edges, edge, width), F32),
        pltpu.VMEM((distinct, width), F32),
        pltpu.VMEM((distinct, width), F32),
        pltpu.VMEM((ITERS, distinct, width), BF16),
        pltpu.VMEM((ITERS, nr, distinct, width), BF16),
        pltpu.VMEM((ITERS, ns, distinct, width), BF16),
        pltpu.VMEM((ITERS, ns, distinct, width), BF16),
        dma((4 * per,)), dma((6,)),
        dma((rounds, edges)), dma((rounds, edges)),
        dma((4,)), dma((4,)),
        dma((edges,)), dma((edges,)),
        dma((nr,)), dma((nr,)),
        dma((ns,)), dma((ns,)),
        dma((ns,)), dma((ns,)),
        dma((nr,)), dma((nr,)),
        dma((1,)), dma((1,)),
        dma((ITERS, nr)), dma((ITERS, nr)),
        dma((ITERS, ns)), dma((ITERS, ns)),
    ]
    out = jax.ShapeDtypeStruct(adjoint_loads.shape, F32)
    kept = pltpu.VMEM(adjoint_loads.shape, F32)
    results = pl.pallas_call(
        functools.partial(kernel, nr, ns),
        out_shape=(kept, kept),
        in_specs=[hbm] * 10,
        out_specs=(vmem, vmem),
        scratch_shapes=scratch,
        compiler_params=pltpu.CompilerParams(
            collective_id=0, has_side_effects=True, vmem_limit_bytes=56 * 1024 * 1024
        ),
    )(*args)
    results = [pltpu.with_memory_space_constraint(x, pltpu.VMEM) for x in results]
    return pl.pallas_call(
        hand_over, out_shape=(out, out), in_specs=[vmem, vmem], out_specs=(hbm, hbm), scratch_shapes=[dma((2,))],
    )(*results)


def solution(mesh):
    placed = (
        P("sx", "sy", None, None, None),
        P("sx", "sy", None, None),
        P("sx", "sy", None, None),
        P("sx", "sy", None, None),
        P("sx", "sy", None, None),
        P("sx", "sy", None, None),
        P("sx", "sy"),
        P("sx", "sy"),
        P("sx", "sy", None),
        P("sx", "sy", None),
    )
    return jax.shard_map(
        functools.partial(local, mesh.shape["sx"], mesh.shape["sy"]),
        mesh=mesh,
        in_specs=placed,
        out_specs=(P("sx", "sy", None, None, None), P("sx", "sy", None, None, None)),
        check_vma=False,
    )
```

```python
import functools

import jax
import jax.numpy as jnp
from jax import lax
from jax.experimental import pallas as pl
from jax.experimental.pallas import tpu as pltpu
from jax.sharding import PartitionSpec as P

ITERS = 2
step_sizes = (0.55, 0.75)
momenta = (0.0, 0.15)

MESH = pl.DeviceIdType.MESH
SLOT = 16
LANES = 128
F32 = jnp.float32
BF16 = jnp.bfloat16
EAST, SOUTH, WEST, NORTH = 0, 1, 2, 3


def sizes_of(nr, ns, per, corners, tr, tc):
    listed = -(-(3 * per + 2) * SLOT // LANES) * LANES
    distinct = -(-(corners // 4) * (4 * per + 8) // SLOT) * SLOT
    pack = 2 if 2 * tc <= LANES and tr % (2 * SLOT) == 0 else 1
    lanes = -(-pack * tc // LANES) * LANES
    return listed, distinct, pack, tr // pack, lanes


def kernel(
    nr, ns,
    loads_in, dual_t, dual_w, diri_t, diri_w, coup_in, cinv_in, wr_in, len_in, cm_in,
    mult_out, prec_out,
    mats, vec, loc, snd, rcv, ld, mu, di,
    lraw, craw, vraw, wr_ref, len_ref, cm_ref,
    meta, nmeta, lens, jcol, dmat, dtm, ub, ux, uz, kp, kmat,
    cedge, cnbr, ce, cet, corr, tdir, tsum, ts, tp, ys, yr,
    mat_sem, in_sem, h_send, h_recv, m_send, m_recv, c_send, c_recv, u_sem, k_sem, t_sem, y_sem,
):
    r, s = lax.axis_index("sx"), lax.axis_index("sy")
    per = loads_in.shape[1]
    edge, width = loads_in.shape[3], loads_in.shape[4]
    corners = coup_in.shape[1]
    tr, tc = cinv_in.shape
    listed, distinct, pack, tp_rows, kl = sizes_of(nr, ns, per, corners, tr, tc)
    rows = per * SLOT
    half = nr // 2
    odd = lax.rem(r, 2)
    has_left, has_right = s > 0, s < ns - 1
    has_up, has_down = r > 0, r < nr - 1
    exists = {EAST: has_right, SOUTH: has_down, WEST: has_left, NORTH: has_up}
    far, near = 3 - 2 * odd, 1 + 2 * odd
    has_far = ((odd == 1) & has_down) | ((odd == 0) & has_up)
    has_near = ((odd == 0) & has_down) | ((odd == 1) & has_up)

    barrier = pltpu.get_barrier_semaphore()
    for k in range(1, nr):
        pl.semaphore_signal(barrier, inc=1, device_id={"sx": lax.rem(r + k, nr)}, device_id_type=MESH)
    for k in range(1, ns):
        pl.semaphore_signal(barrier, inc=1, device_id={"sy": lax.rem(s + k, ns)}, device_id_type=MESH)

    small = [
        pltpu.make_async_copy(src, dst, in_sem.at[i])
        for i, (src, dst) in enumerate(
            ((wr_in, wr_ref), (len_in, len_ref), (cm_in, cm_ref), (loads_in.at[0], lraw), (coup_in.at[0], craw), (cinv_in, vraw))
        )
    ]
    for copy in small:
        copy.start()
    am, aw, bm, bw = 0, 1, 2, 3

    def fetch(c, first, act):
        if act == "start":
            for i, src in enumerate((diri_t, diri_w) if first == am else (dual_t, dual_w)):
                pltpu.make_async_copy(src.at[0, c], mats.at[c, first + i], mat_sem.at[c]).start()
        else:
            both = mats.at[c, first : first + 2]
            pltpu.make_async_copy(both, both, mat_sem.at[c]).wait()

    positions = lax.broadcasted_iota(jnp.int32, (edge, width), 0)

    def live(row):
        return positions < jnp.broadcast_to(row, (edge, width))

    def mask_of(i):
        return live(lens[pl.ds(i, 1), :])

    def at_edge(c, e):
        return e * per + c

    def rows_of(e):
        return pl.ds(pl.multiple_of(e * edge, SLOT), edge)

    def put(c, e, value):
        vec[c, rows_of(e)] = value.astype(BF16)

    def pieces(e):
        if isinstance(e, int) and e in (EAST, WEST):
            here, there = (per - 1, 0) if e == EAST else (0, per - 1)
            return pl.ds(e * per + here, 1), pl.ds((2 - e) * per + there, 1)
        return pl.ds(e * per, per), pl.ds((4 - e) * per, per)

    def neighbour(e):
        return {"sy": s + (1 - e)} if isinstance(e, int) and e in (EAST, WEST) else {"sx": r + (2 - e)}

    def opposite(e):
        return 2 - e if isinstance(e, int) and e in (EAST, WEST) else 4 - e

    def xfer(k, e):
        here, there = pieces(e)
        return pltpu.make_async_remote_copy(
            src_ref=snd.at[k, here], dst_ref=rcv.at[k, there], send_sem=h_send.at[e], recv_sem=h_recv.at[k % 2, opposite(e)],
            device_id=neighbour(e), device_id_type=MESH,
        )

    def ship(k, e, there):
        @pl.when(there)
        def _():
            xfer(k, e).start()

    def taken(ref, sem):
        pltpu.make_async_copy(ref, ref, sem).wait()

    def arrive(k, e, there):
        @pl.when(there)
        def _():
            taken(rcv.at[k, pieces(e)[0]], h_recv.at[k % 2, e])

    def peers(axis, src, dst, sems):
        n, me = (nr, r) if axis == "sx" else (ns, s)
        out = []
        for k in range(1, n):
            to = lax.rem(me + k, n)
            out.append(
                pltpu.make_async_remote_copy(
                    src_ref=src(to), dst_ref=dst, send_sem=sems.at[0], recv_sem=sems.at[1],
                    device_id={axis: to}, device_id_type=MESH,
                )
            )
        return out

    def meta_copy(e):
        return pltpu.make_async_remote_copy(
            src_ref=meta, dst_ref=nmeta.at[opposite(e)], send_sem=m_send.at[e], recv_sem=m_recv.at[opposite(e)],
            device_id=neighbour(e), device_id_type=MESH,
        )

    def coupling_copy(e):
        here, there = pieces(e)
        return pltpu.make_async_remote_copy(
            src_ref=cedge.at[here], dst_ref=cnbr.at[there], send_sem=c_send.at[e], recv_sem=c_recv.at[opposite(e)],
            device_id=neighbour(e), device_id_type=MESH,
        )

    shared = [(c, SOUTH) for c in range(per)] + [(c, NORTH) for c in range(per)] + [(per - 1, EAST), (0, WEST)]

    for copy in small[:3]:
        copy.wait()
    for c in range(per):
        fetch(c, am, "start")
    meta[...] = jnp.full(meta.shape, -1, jnp.int32)
    for c in range(per):
        for m in range(corners):
            meta[c * SLOT + m : c * SLOT + m + 1, :] = jnp.full((1, LANES), cm_ref[0, c, m], jnp.int32)
        east = len_ref[0, c, 0]
        if c == per - 1:
            east = jnp.where(has_right, east, 0)
        south = jnp.where(has_down, len_ref[0, c, 1], 0)
        for e, length in ((EAST, east), (SOUTH, south)):
            row = jnp.full((1, LANES), length, jnp.int32)
            meta[rows + 2 * c + e : rows + 2 * c + e + 1, :] = row
            lens[at_edge(c, e) : at_edge(c, e) + 1, :] = row
    small[3].wait()
    for c in range(per):
        for e in (EAST, SOUTH):
            value = jnp.where(live(lens[at_edge(c, e) : at_edge(c, e) + 1, :]), lraw[c, e], 0.0)
            ld[at_edge(c, e)] = value
            put(c, e, 0.5 * value)
            if e == SOUTH or c == per - 1:
                snd[0, at_edge(c, e)] = value.astype(BF16)
            else:
                put(c + 1, WEST, -0.5 * value)

    small[5].wait()
    tile = vraw[...].astype(F32)
    parts = [tile[h * tp_rows : (h + 1) * tp_rows] for h in range(pack)]
    if kl > pack * tc:
        parts.append(jnp.zeros((tp_rows, kl - pack * tc), F32))
    kp[odd, lax.div(r, 2), s] = jnp.concatenate(parts, axis=1).astype(BF16)
    mine = kp.at[odd, lax.div(r, 2)]
    k1 = peers("sy", lambda to: mine.at[s], mine.at[s], k_sem.at[0])
    k2 = [
        pltpu.make_async_remote_copy(
            src_ref=mine, dst_ref=mine, send_sem=k_sem.at[1, 0], recv_sem=k_sem.at[1, 1],
            device_id={"sx": lax.rem(r + 2 * k, nr)}, device_id_type=MESH,
        )
        for k in range(1, half)
    ]
    k3 = pltpu.make_async_remote_copy(
        src_ref=kp.at[odd], dst_ref=kp.at[odd], send_sem=k_sem.at[2, 0], recv_sem=k_sem.at[2, 1],
        device_id={"sx": r + 1 - 2 * odd}, device_id_type=MESH,
    )
    pl.semaphore_wait(barrier, nr - 1 + ns - 1)
    for e in range(4):
        @pl.when(exists[e])
        def _(e=e):
            meta_copy(e).start()
    for copy in k1:
        copy.start()
    ship(0, SOUTH, has_down)
    ship(0, EAST, has_right)
    small[4].wait()
    for c in range(per):
        whole = jnp.concatenate(
            [craw[:, c, :].astype(F32), jnp.zeros((SLOT - corners, craw.shape[2]), F32)], axis=0
        )
        turned = whole.T
        for e in range(4):
            cedge[at_edge(c, e)] = turned[e * edge : (e + 1) * edge].T.astype(BF16)
    for e in range(4):
        @pl.when(exists[e])
        def _(e=e):
            coupling_copy(e).start()

    def combine(c, main):
        flag = jnp.full((1, 1), wr_ref[0, c], jnp.int32).astype(F32).astype(BF16)
        size = mats.shape[2]
        step = 128

        def body(i, _):
            part = pl.ds(pl.multiple_of(i * step, step), step)
            mats[c, main, part] = mats[c, main, part] + flag * mats[c, main + 1, part]
            return 0

        lax.fori_loop(0, size // step, body, 0)

    def ready(c):
        fetch(c, am, "wait")
        fetch(c, bm, "start")
        combine(c, am)

    ready(0)

    for e in range(4):
        @pl.when(exists[e])
        def _(e=e):
            taken(nmeta.at[e], m_recv.at[e])
    for c in range(per):
        row = nmeta[NORTH, rows + 2 * c + SOUTH : rows + 2 * c + SOUTH + 1, :]
        lens[at_edge(c, NORTH) : at_edge(c, NORTH) + 1, :] = jnp.where(has_up, row, 0)
    row = nmeta[WEST, rows + 2 * (per - 1) + EAST : rows + 2 * (per - 1) + EAST + 1, :]
    lens[at_edge(0, WEST) : at_edge(0, WEST) + 1, :] = jnp.where(has_left, row, 0)

    place = {}
    jcol[...] = jnp.full(jcol.shape, -1, jnp.int32)
    for c in range(per):
        jcol[c * SLOT : (c + 1) * SLOT, :] = meta[c * SLOT : (c + 1) * SLOT, :]
    for i, (c, e) in enumerate(shared):
        place[c, e] = (per + i) * SLOT
        theirs = (0 if e == EAST else per - 1 if e == WEST else c) * SLOT
        jcol[place[c, e] : place[c, e] + SLOT, :] = jnp.where(exists[e], nmeta[e, theirs : theirs + SLOT, :], -1)
    for c in range(per - 1):
        place[c, EAST] = (c + 1) * SLOT
    square = (listed, listed)
    jf = jnp.broadcast_to(jcol[:, 0:1], square).astype(F32)
    jr = jf.T
    row_id = lax.broadcasted_iota(jnp.int32, square, 0)
    lane_id = lax.broadcasted_iota(jnp.int32, square, 1)
    again = jnp.max(jnp.where((jf == jr) & (lane_id < row_id), 1.0, 0.0), axis=1, keepdims=True)
    first = jnp.where(jf[:, 0:1] >= 0.0, 1.0 - again, 0.0)
    first_row = jnp.broadcast_to(first, square).T
    rank = jnp.sum(jnp.where(lane_id < row_id, first_row, 0.0), axis=1, keepdims=True)
    chosen = (jnp.broadcast_to(rank, square) == lane_id.astype(F32)) & (jnp.broadcast_to(first, square) > 0.5)
    u_row = jnp.sum(jnp.where(chosen, jf + 1.0, 0.0), axis=0, keepdims=True) - 1.0
    u_lanes = jnp.broadcast_to(u_row, square)
    u_rows = u_lanes.T
    dmat[...] = jnp.where((u_rows == jr) & (jr >= 0.0), 1.0, 0.0)[0:distinct].astype(BF16)
    dtm[...] = jnp.where((jf == u_lanes) & (jf >= 0.0), 1.0, 0.0)[:, 0:distinct].astype(BF16)
    u_block = jnp.broadcast_to(u_row, ub.shape).astype(jnp.int32)
    ub[...] = u_block
    ux[pl.ds(r, 1)] = u_block[None]
    uz[pl.ds(s, 1)] = u_block[None]
    uxc = peers("sx", lambda to: ub, ux.at[r], u_sem.at[0])
    uzc = peers("sy", lambda to: ub, uz.at[s], u_sem.at[1])
    for copy in uxc + uzc:
        copy.start()

    for c in range(1, per):
        ready(c)

    for e in range(4):
        @pl.when(exists[e])
        def _(e=e):
            taken(cnbr.at[pieces(e)[0]], c_recv.at[e])
    for c, e in place:
        if (c, e) in shared:
            theirs = jnp.where(exists[e], cnbr[at_edge(c, e)].astype(F32), 0.0)
        else:
            theirs = cedge[at_edge(c + 1, WEST)].astype(F32)
        both = jnp.concatenate([cedge[at_edge(c, e)].astype(F32), -theirs], axis=0)
        column = lax.broadcasted_iota(jnp.int32, both.shape, 1)
        length = jnp.broadcast_to(lens[at_edge(c, e) : at_edge(c, e) + 1, 0:1], both.shape)
        ce[at_edge(c, e)] = jnp.where(column < length, both, 0.0).astype(BF16)

    def setup_turned():
        for c, e in place:
            cet[at_edge(c, e)] = ce[at_edge(c, e)].astype(F32).T.astype(BF16)

    def setup_coarse():
        taken(ux.at[0 : nr - 1], u_sem.at[0, 1])
        taken(uz.at[0 : ns - 1], u_sem.at[1, 1])
        k3.wait_recv()
        count = ns * distinct
        wanted = jnp.concatenate(
            [jnp.broadcast_to(uz[q, 0:1, :].astype(F32), square).T[0:distinct, 0:1] for q in range(ns)], axis=0
        )
        at = lax.broadcasted_iota(jnp.int32, (8, nr * tp_rows), 1)
        index = at
        start = [(2 * (m % half) + m // half) * tr for m in range(nr)]
        for m in range(1, nr):
            jump = (start[m] - m * tp_rows) - (start[m - 1] - (m - 1) * tp_rows)
            index = index + jnp.where(at >= m * tp_rows, jump, 0)
        index = index.astype(F32)[0:1]
        lane = lax.broadcasted_iota(jnp.int32, (count, kl), 1)
        picks = [
            jnp.where(
                jnp.broadcast_to(wanted, (count, nr * tp_rows)) == jnp.broadcast_to(index + h * tp_rows, (count, nr * tp_rows)),
                1.0, 0.0,
            ).astype(BF16)
            for h in range(pack)
        ]
        chosen_rows = []
        for q in range(ns):
            plane = kp[:, :, q].astype(F32).reshape(nr * tp_rows, kl).astype(BF16)
            total = jnp.zeros((count, kl), F32)
            for h in range(pack):
                found = jnp.dot(picks[h], plane, preferred_element_type=F32)
                total = jnp.where((lane >= h * tc) & (lane < (h + 1) * tc), found, total)
            chosen_rows.append(total.astype(BF16))
        chosen_rows = jnp.concatenate(chosen_rows, axis=1)
        deep = lax.broadcasted_iota(jnp.int32, (ns * kl, nr * distinct), 0)
        column = jnp.full((ns * kl, nr * distinct), -5, jnp.int32)
        for q in range(ns):
            for h in range(pack):
                low = q * kl + h * tc
                column = jnp.where((deep >= low) & (deep < low + tc), deep - low + q * tc, column)
        listing = jnp.concatenate([ux[q, 0:1, 0:distinct] for q in range(nr)], axis=1)
        pick = jnp.where(column == jnp.broadcast_to(listing, column.shape), 1.0, 0.0).astype(BF16)
        kmat[...] = jnp.dot(chosen_rows, pick, preferred_element_type=F32).astype(BF16)

    def products(k, mat, what):
        for c, e, sent in what:
            value = jnp.dot(mats[c, mat, rows_of(e), :], vec[c], preferred_element_type=F32)
            loc[c, rows_of(e)] = value
            if sent:
                snd[k, at_edge(c, e)] = value.astype(BF16)

    def own(c, e):
        return loc[c, rows_of(e)]

    far_edges = [(c, far, True) for c in range(per)]
    near_edges = [(c, near, True) for c in range(per)]
    inner_blocks = [(c, EAST, False) for c in range(per - 1)] + [(c, WEST, False) for c in range(1, per)]

    sides = [(0, WEST, True), (per - 1, EAST, True)]

    def apply_m(k):
        products(k, am, far_edges)
        ship(k, far, has_far)
        products(k, am, sides)
        ship(k, WEST, has_left)
        ship(k, EAST, has_right)
        products(k, am, near_edges + inner_blocks)
        ship(k, near, has_near)

    def apply_f(k, between, late):
        products(k, bm, far_edges)
        ship(k, far, has_far)
        if late:
            products(k, bm, sides)
        between()
        if not late:
            products(k, bm, sides)
        ship(k, WEST, has_left)
        ship(k, EAST, has_right)
        products(k, bm, near_edges + inner_blocks)
        ship(k, near, has_near)

    def gathered(k, c, e):
        return own(c, e) - rcv[k, at_edge(c, e)].astype(F32)

    def exchanged(k, act):
        for c in range(per - 1):
            act(c, EAST, own(c, EAST) - own(c + 1, WEST))
        arrive(k, near, has_near)
        for c in range(per):
            act(c, near, gathered(k, c, near))
        for c, e in ((0, WEST), (per - 1, EAST)):
            arrive(k, e, exists[e])
            act(c, e, gathered(k, c, e))
        arrive(k, far, has_far)
        for c in range(per):
            act(c, far, gathered(k, c, far))

    def is_inner(c, e):
        return isinstance(e, int) and e == EAST and c < per - 1

    arrive(0, WEST, has_left)
    value = jnp.where(jnp.broadcast_to(has_left, (edge, width)), -rcv[0, at_edge(0, WEST)].astype(F32), 0.0)
    ld[at_edge(0, WEST)] = value
    put(0, WEST, 0.5 * value)
    arrive(0, NORTH, has_up)
    for c in range(per):
        value = jnp.where(jnp.broadcast_to(has_up, (edge, width)), -rcv[0, at_edge(c, NORTH)].astype(F32), 0.0)
        ld[at_edge(c, NORTH)] = value
        put(c, NORTH, 0.5 * value)

    taken(mine.at[0 : ns - 1], k_sem.at[0, 1])
    for copy in k2:
        copy.start()

    halo_round = 1
    for number in range(ITERS):
        apply_m(halo_round)

        acc = [jnp.zeros((SLOT, width), F32) for _ in range(listed // SLOT)]
        for (c, e), at in place.items():
            if is_inner(c, e):
                value = (own(c, e) - own(c + 1, WEST)).astype(BF16)
            else:
                value = snd[halo_round, at_edge(c, e)]
            both = jnp.dot(ce[at_edge(c, e)], value, preferred_element_type=F32)
            acc[c] = acc[c] + both[0:SLOT]
            acc[at // SLOT] = acc[at // SLOT] + both[SLOT:]
        terms = 0.5 * jnp.concatenate(acc, axis=0)
        high = terms.astype(BF16)
        low = (terms - high.astype(F32)).astype(BF16)
        terms = jnp.dot(dmat[...], high, preferred_element_type=F32) + jnp.dot(dmat[...], low, preferred_element_type=F32)
        if number > 0:
            terms = terms + momenta[number] * tdir[...]
        tdir[...] = terms
        terms = step_sizes[number] * terms
        if number > 0:
            terms = terms + tsum[...]
        tsum[...] = terms
        terms = terms.astype(BF16)
        ts[number] = terms
        tp[number, pl.ds(r, 1)] = terms[None]
        tcopies = peers("sx", lambda to: ts.at[number], tp.at[number, r], t_sem.at[number])
        for copy in tcopies:
            copy.start()

        if number == 0:
            for c in range(per):
                fetch(c, bm, "wait")
                combine(c, bm)
                if c == 0:
                    taken(kp.at[odd, 0 : half - 1], k_sem.at[1, 1])
                    k3.start()
            setup_turned()
            setup_coarse()

        def advance(c, e, value):
            i = at_edge(c, e)
            value = jnp.where(mask_of(i), 0.5 * value, 0.0)
            if number == 0:
                iterate = step_sizes[0] * value
            else:
                value = value + momenta[number] * di[i]
                iterate = mu[i] + step_sizes[number] * value
            if number < ITERS - 1:
                di[i] = value
            mu[i] = iterate
            put(c, e, iterate)
            if is_inner(c, e):
                put(c + 1, WEST, -iterate)

        exchanged(halo_round, advance)
        halo_round += 1

        ycopies = peers("sy", lambda to: ys.at[number, to], yr.at[number, s], y_sem.at[number])

        def coarse():
            taken(tp.at[number, 0 : nr - 1], t_sem.at[number, 1])
            partial = jnp.dot(kmat[...], tp[number].reshape(nr * distinct, width), preferred_element_type=F32)
            ys[number] = partial.astype(BF16).reshape(ns, distinct, width)
            yr[number, pl.ds(s, 1)] = ys[number, pl.ds(s, 1)]
            for copy in ycopies:
                copy.start()

        apply_f(halo_round, coarse, number > 0)
        if number == ITERS - 1:
            for c in range(per):
                for e in (EAST, SOUTH):
                    mult_out[0, c, e] = mu[at_edge(c, e)]
        taken(yr.at[number, 0 : ns - 1], y_sem.at[number, 1])
        solved = yr[number, 0].astype(F32)
        for q in range(1, ns):
            solved = solved + yr[number, q].astype(F32)
        solved = jnp.dot(dtm[...], solved.astype(BF16), preferred_element_type=F32)
        for (c, e), at in place.items():
            both = jnp.concatenate([solved[c * SLOT : (c + 1) * SLOT], solved[at : at + SLOT]], axis=0).astype(BF16)
            corr[at_edge(c, e)] = jnp.dot(cet[at_edge(c, e)], both, preferred_element_type=F32)

        def remain(c, e, value):
            i = at_edge(c, e)
            value = 0.5 * (ld[i] - jnp.where(mask_of(i), value + corr[i], 0.0))
            put(c, e, value)
            if is_inner(c, e):
                put(c + 1, WEST, -value)

        exchanged(halo_round, remain)
        halo_round += 1

    products(halo_round, am, [(c, NORTH, True) for c in range(per)])
    ship(halo_round, NORTH, has_up)
    products(halo_round, am, [(0, WEST, True)])
    ship(halo_round, WEST, has_left)
    products(
        None, am, [(c, e, False) for c in range(per) for e in (EAST, SOUTH)] + [(c, WEST, False) for c in range(1, per)]
    )

    def finish(c, e, value):
        prec_out[0, c, e] = jnp.where(mask_of(at_edge(c, e)), 0.5 * value, 0.0)

    for c in range(per - 1):
        finish(c, EAST, own(c, EAST) - own(c + 1, WEST))
    arrive(halo_round, EAST, has_right)
    finish(per - 1, EAST, gathered(halo_round, per - 1, EAST))
    arrive(halo_round, SOUTH, has_down)
    for c in range(per):
        finish(c, SOUTH, gathered(halo_round, c, SOUTH))

    for e in range(4):
        @pl.when(exists[e])
        def _(e=e):
            meta_copy(e).wait_send()
            coupling_copy(e).wait_send()
            taken(snd.at[0:halo_round, pieces(e)[0]], h_send.at[e])
    taken(mine.at[0 : ns - 1], k_sem.at[0, 0])
    taken(kp.at[odd, 0 : half - 1], k_sem.at[1, 0])
    k3.wait_send()
    taken(ux.at[0 : nr - 1], u_sem.at[0, 0])
    taken(uz.at[0 : ns - 1], u_sem.at[1, 0])
    for number in range(ITERS):
        taken(tp.at[number, 0 : nr - 1], t_sem.at[number, 0])
        taken(yr.at[number, 0 : ns - 1], y_sem.at[number, 0])


def hand_over(mult_in, prec_in, mult_out, prec_out, sem):
    copies = [
        pltpu.make_async_copy(mult_in, mult_out, sem.at[0]),
        pltpu.make_async_copy(prec_in, prec_out, sem.at[1]),
    ]
    for copy in copies:
        copy.start()
    for copy in copies:
        copy.wait()


def local(nr, ns, *args):
    adjoint_loads, dual_taut, coupling, coarse_inverse = args[0], args[1], args[5], args[6]
    per, edge, width = adjoint_loads.shape[1], adjoint_loads.shape[3], adjoint_loads.shape[4]
    size = dual_taut.shape[-1]
    corners = coupling.shape[2]
    tr, tc = coarse_inverse.shape
    listed, distinct, pack, tp_rows, kl = sizes_of(nr, ns, per, corners, tr, tc)
    rows = per * SLOT
    rounds = 2 * ITERS + 2
    edges = 4 * per
    meta_rows = rows + -(-2 * per // 8) * 8
    dma = pltpu.SemaphoreType.DMA
    vmem = pl.BlockSpec(memory_space=pltpu.VMEM)
    hbm = pl.BlockSpec(memory_space=pl.ANY)
    args = args[:5] + (jnp.transpose(coupling, (0, 2, 1, 3)),) + args[6:]
    i32 = jnp.int32
    scratch = [
        pltpu.VMEM((per, 4, size, size), BF16),
        pltpu.VMEM((per, size, width), BF16),
        pltpu.VMEM((per, size, width), F32),
        pltpu.VMEM((rounds, edges, edge, width), BF16),
        pltpu.VMEM((rounds, edges, edge, width), BF16),
        pltpu.VMEM((edges, edge, width), F32),
        pltpu.VMEM((edges, edge, width), F32),
        pltpu.VMEM((edges, edge, width), F32),
        pltpu.VMEM(adjoint_loads.shape[1:], F32),
        pltpu.VMEM(args[5].shape[1:], BF16),
        pltpu.VMEM((tr, tc), BF16),
        pltpu.SMEM(args[7].shape, i32),
        pltpu.SMEM(args[8].shape, i32),
        pltpu.SMEM(args[9].shape, i32),
        pltpu.VMEM((meta_rows, LANES), i32),
        pltpu.VMEM((4, meta_rows, LANES), i32),
        pltpu.VMEM((-(-edges // 8) * 8, LANES), i32),
        pltpu.VMEM((listed, LANES), i32),
        pltpu.VMEM((distinct, listed), BF16),
        pltpu.VMEM((listed, distinct), BF16),
        pltpu.VMEM((8, listed), i32),
        pltpu.VMEM((nr, 8, listed), i32),
        pltpu.VMEM((ns, 8, listed), i32),
        pltpu.VMEM((2, nr // 2, ns, tp_rows, kl), BF16),
        pltpu.VMEM((ns * distinct, nr * distinct), BF16),
        pltpu.VMEM((edges, SLOT, edge), BF16),
        pltpu.VMEM((edges, SLOT, edge), BF16),
        pltpu.VMEM((edges, 2 * SLOT, edge), BF16),
        pltpu.VMEM((edges, edge, 2 * SLOT), BF16),
        pltpu.VMEM((edges, edge, width), F32),
        pltpu.VMEM((distinct, width), F32),
        pltpu.VMEM((distinct, width), F32),
        pltpu.VMEM((ITERS, distinct, width), BF16),
        pltpu.VMEM((ITERS, nr, distinct, width), BF16),
        pltpu.VMEM((ITERS, ns, distinct, width), BF16),
        pltpu.VMEM((ITERS, ns, distinct, width), BF16),
        dma((per,)), dma((6,)),
        dma((4,)), dma((2, 4)),
        dma((4,)), dma((4,)),
        dma((4,)), dma((4,)),
        dma((2, 2)), dma((3, 2)), dma((ITERS, 2)), dma((ITERS, 2)),
    ]
    out = jax.ShapeDtypeStruct(adjoint_loads.shape, F32)
    kept = pltpu.VMEM(adjoint_loads.shape, F32)
    results = pl.pallas_call(
        functools.partial(kernel, nr, ns),
        out_shape=(kept, kept),
        in_specs=[hbm] * 10,
        out_specs=(vmem, vmem),
        scratch_shapes=scratch,
        compiler_params=pltpu.CompilerParams(
            collective_id=0, has_side_effects=True, vmem_limit_bytes=56 * 1024 * 1024
        ),
    )(*args)
    results = [pltpu.with_memory_space_constraint(x, pltpu.VMEM) for x in results]
    return pl.pallas_call(
        hand_over, out_shape=(out, out), in_specs=[vmem, vmem], out_specs=(hbm, hbm), scratch_shapes=[dma((2,))],
    )(*results)


def solution(mesh):
    placed = (
        P("sx", "sy", None, None, None),
        P("sx", "sy", None, None),
        P("sx", "sy", None, None),
        P("sx", "sy", None, None),
        P("sx", "sy", None, None),
        P("sx", "sy", None, None),
        P("sx", "sy"),
        P("sx", "sy"),
        P("sx", "sy", None),
        P("sx", "sy", None),
    )
    return jax.shard_map(
        functools.partial(local, mesh.shape["sx"], mesh.shape["sy"]),
        mesh=mesh,
        in_specs=placed,
        out_specs=(P("sx", "sy", None, None, None), P("sx", "sy", None, None, None)),
        check_vma=False,
    )
```

```python
import functools

import jax
import jax.numpy as jnp
from jax import lax
from jax.experimental import pallas as pl
from jax.experimental.pallas import tpu as pltpu
from jax.sharding import PartitionSpec as P

ITERS = 2
step_sizes = (0.55, 0.75)
momenta = (0.0, 0.15)

MESH = pl.DeviceIdType.MESH
SLOT = 16
LANES = 128
F32 = jnp.float32
BF16 = jnp.bfloat16
EAST, SOUTH, WEST, NORTH = 0, 1, 2, 3


def sizes_of(nr, ns, per, corners, tr, tc):
    listed = -(-(3 * per + 2) * SLOT // LANES) * LANES
    distinct = -(-(corners // 4) * (4 * per + 8) // SLOT) * SLOT
    pack = 2 if 2 * tc <= LANES and tr % (2 * SLOT) == 0 else 1
    lanes = -(-pack * tc // LANES) * LANES
    return listed, distinct, pack, tr // pack, lanes


def kernel(
    nr, ns,
    loads_in, dual_t, dual_w, diri_t, diri_w, coup_in, cinv_in, wr_in, len_in, cm_in,
    mult_out, prec_out,
    mats, vec, loc, snd, rcv, ld, mu, di,
    lraw, craw, vraw, wr_ref, len_ref, cm_ref,
    meta, nmeta, lens, jcol, dmat, dtm, ub, ux, uz, kp, kmat,
    cedge, cnbr, ce, em, gm, sol, tdir, tsum, ts, tp, ys, yr,
    mat_sem, in_sem, h_send, h_recv, m_send, m_recv, c_send, c_recv, u_sem, k_sem, t_sem, y_sem,
):
    r, s = lax.axis_index("sx"), lax.axis_index("sy")
    per = loads_in.shape[1]
    edge, width = loads_in.shape[3], loads_in.shape[4]
    corners = coup_in.shape[1]
    tr, tc = cinv_in.shape
    listed, distinct, pack, tp_rows, kl = sizes_of(nr, ns, per, corners, tr, tc)
    rows = per * SLOT
    half = nr // 2
    odd = lax.rem(r, 2)
    has_left, has_right = s > 0, s < ns - 1
    has_up, has_down = r > 0, r < nr - 1
    exists = {EAST: has_right, SOUTH: has_down, WEST: has_left, NORTH: has_up}
    far, near = 3 - 2 * odd, 1 + 2 * odd
    has_far = ((odd == 1) & has_down) | ((odd == 0) & has_up)
    has_near = None if nr % 2 == 0 else ((odd == 0) & has_down) | ((odd == 1) & has_up)

    barrier = pltpu.get_barrier_semaphore()
    for k in range(1, nr):
        pl.semaphore_signal(barrier, inc=1, device_id={"sx": lax.rem(r + k, nr)}, device_id_type=MESH)
    for k in range(1, ns):
        pl.semaphore_signal(barrier, inc=1, device_id={"sy": lax.rem(s + k, ns)}, device_id_type=MESH)

    small = [
        pltpu.make_async_copy(src, dst, in_sem.at[i])
        for i, (src, dst) in enumerate(
            ((wr_in, wr_ref), (len_in, len_ref), (cm_in, cm_ref), (loads_in.at[0], lraw), (coup_in.at[0], craw), (cinv_in, vraw))
        )
    ]
    for copy in small:
        copy.start()
    am, aw, bm, bw = 0, 1, 2, 3

    def fetch(c, first, act):
        if act == "start":
            for i, src in enumerate((diri_t, diri_w) if first == am else (dual_t, dual_w)):
                pltpu.make_async_copy(src.at[0, c], mats.at[c, first + i], mat_sem.at[c]).start()
        else:
            both = mats.at[c, first : first + 2]
            pltpu.make_async_copy(both, both, mat_sem.at[c]).wait()

    positions = lax.broadcasted_iota(jnp.int32, (edge, width), 0)

    def live(row):
        return positions < jnp.broadcast_to(row, (edge, width))

    def mask_of(i):
        return live(lens[pl.ds(i, 1), :])

    def at_edge(c, e):
        return e * per + c

    def rows_of(e):
        return pl.ds(pl.multiple_of(e * edge, SLOT), edge)

    def put(c, e, value):
        vec[c, rows_of(e)] = value.astype(BF16)

    def pieces(e):
        if isinstance(e, int) and e in (EAST, WEST):
            here, there = (per - 1, 0) if e == EAST else (0, per - 1)
            return pl.ds(e * per + here, 1), pl.ds((2 - e) * per + there, 1)
        return pl.ds(e * per, per), pl.ds((4 - e) * per, per)

    def neighbour(e):
        return {"sy": s + (1 - e)} if isinstance(e, int) and e in (EAST, WEST) else {"sx": r + (2 - e)}

    def opposite(e):
        return 2 - e if isinstance(e, int) and e in (EAST, WEST) else 4 - e

    def xfer(k, e):
        here, there = pieces(e)
        return pltpu.make_async_remote_copy(
            src_ref=snd.at[k, here], dst_ref=rcv.at[k, there], send_sem=h_send.at[e], recv_sem=h_recv.at[k % 2, opposite(e)],
            device_id=neighbour(e), device_id_type=MESH,
        )

    def ship(k, e, there):
        here, land = pieces(e)
        size = edge // 1

        def go():
            for c in range(here.size):
                for i in range(1):
                    some = pl.ds(i * size, size)
                    pltpu.make_async_remote_copy(
                        src_ref=snd.at[k, here.start + c, some], dst_ref=rcv.at[k, land.start + c, some],
                        send_sem=h_send.at[e], recv_sem=h_recv.at[k % 2, opposite(e)],
                        device_id=neighbour(e), device_id_type=MESH,
                    ).start()

        if there is None:
            go()
        else:
            pl.when(there)(go)

    def taken(ref, sem):
        pltpu.make_async_copy(ref, ref, sem).wait()

    def arrive(k, e, there):
        if there is None:
            taken(rcv.at[k, pieces(e)[0]], h_recv.at[k % 2, e])
        else:
            pl.when(there)(lambda: taken(rcv.at[k, pieces(e)[0]], h_recv.at[k % 2, e]))

    def peers(axis, src, dst, sems):
        n, me = (nr, r) if axis == "sx" else (ns, s)
        out = []
        for k in range(1, n):
            to = lax.rem(me + k, n)
            out.append(
                pltpu.make_async_remote_copy(
                    src_ref=src(to), dst_ref=dst, send_sem=sems.at[0], recv_sem=sems.at[1],
                    device_id={axis: to}, device_id_type=MESH,
                )
            )
        return out

    def meta_copy(e):
        return pltpu.make_async_remote_copy(
            src_ref=meta, dst_ref=nmeta.at[opposite(e)], send_sem=m_send.at[e], recv_sem=m_recv.at[opposite(e)],
            device_id=neighbour(e), device_id_type=MESH,
        )

    def coupling_copy(e):
        here, there = pieces(e)
        return pltpu.make_async_remote_copy(
            src_ref=cedge.at[here], dst_ref=cnbr.at[there], send_sem=c_send.at[e], recv_sem=c_recv.at[opposite(e)],
            device_id=neighbour(e), device_id_type=MESH,
        )

    shared = [(c, SOUTH) for c in range(per)] + [(c, NORTH) for c in range(per)] + [(per - 1, EAST), (0, WEST)]

    for copy in small[:3]:
        copy.wait()
    for c in range(per):
        fetch(c, am, "start")
    meta[...] = jnp.full(meta.shape, -1, jnp.int32)
    for c in range(per):
        for m in range(corners):
            meta[c * SLOT + m : c * SLOT + m + 1, :] = jnp.full((1, LANES), cm_ref[0, c, m], jnp.int32)
        east = len_ref[0, c, 0]
        if c == per - 1:
            east = jnp.where(has_right, east, 0)
        south = jnp.where(has_down, len_ref[0, c, 1], 0)
        for e, length in ((EAST, east), (SOUTH, south)):
            row = jnp.full((1, LANES), length, jnp.int32)
            meta[rows + 2 * c + e : rows + 2 * c + e + 1, :] = row
            lens[at_edge(c, e) : at_edge(c, e) + 1, :] = row
    small[3].wait()
    for c in range(per):
        for e in (EAST, SOUTH):
            value = jnp.where(live(lens[at_edge(c, e) : at_edge(c, e) + 1, :]), lraw[c, e], 0.0)
            ld[at_edge(c, e)] = value
            put(c, e, 0.5 * value)
            if e == SOUTH or c == per - 1:
                snd[0, at_edge(c, e)] = value.astype(BF16)
            else:
                put(c + 1, WEST, -0.5 * value)

    small[5].wait()
    tile = vraw[...].astype(F32)
    parts = [tile[h * tp_rows : (h + 1) * tp_rows] for h in range(pack)]
    if kl > pack * tc:
        parts.append(jnp.zeros((tp_rows, kl - pack * tc), F32))
    kp[odd, lax.div(r, 2), s] = jnp.concatenate(parts, axis=1).astype(BF16)
    mine = kp.at[odd, lax.div(r, 2)]
    k1 = peers("sy", lambda to: mine.at[s], mine.at[s], k_sem.at[0])
    k2 = [
        pltpu.make_async_remote_copy(
            src_ref=mine, dst_ref=mine, send_sem=k_sem.at[1, 0], recv_sem=k_sem.at[1, 1],
            device_id={"sx": lax.rem(r + 2 * k, nr)}, device_id_type=MESH,
        )
        for k in range(1, half)
    ]
    k3 = pltpu.make_async_remote_copy(
        src_ref=kp.at[odd], dst_ref=kp.at[odd], send_sem=k_sem.at[2, 0], recv_sem=k_sem.at[2, 1],
        device_id={"sx": r + 1 - 2 * odd}, device_id_type=MESH,
    )
    pl.semaphore_wait(barrier, nr - 1 + ns - 1)
    for e in range(4):
        @pl.when(exists[e])
        def _(e=e):
            meta_copy(e).start()
    for copy in k1:
        copy.start()
    ship(0, SOUTH, has_down)
    ship(0, EAST, has_right)
    small[4].wait()
    for c in range(per):
        whole = jnp.concatenate(
            [craw[:, c, :].astype(F32), jnp.zeros((SLOT - corners, craw.shape[2]), F32)], axis=0
        )
        turned = whole.T
        for e in range(4):
            cedge[at_edge(c, e)] = turned[e * edge : (e + 1) * edge].T.astype(BF16)
    for e in range(4):
        @pl.when(exists[e])
        def _(e=e):
            coupling_copy(e).start()

    def combine(c, main):
        flag = jnp.full((1, 1), wr_ref[0, c], jnp.int32).astype(F32).astype(BF16)
        size = mats.shape[2]
        step = 128

        def body(i, _):
            part = pl.ds(pl.multiple_of(i * step, step), step)
            mats[c, main, part] = mats[c, main, part] + flag * mats[c, main + 1, part]
            return 0

        lax.fori_loop(0, size // step, body, 0)

    def ready(c):
        fetch(c, am, "wait")
        fetch(c, bm, "start")
        combine(c, am)

    ready(0)

    for e in range(4):
        @pl.when(exists[e])
        def _(e=e):
            taken(nmeta.at[e], m_recv.at[e])
    for c in range(per):
        row = nmeta[NORTH, rows + 2 * c + SOUTH : rows + 2 * c + SOUTH + 1, :]
        lens[at_edge(c, NORTH) : at_edge(c, NORTH) + 1, :] = jnp.where(has_up, row, 0)
    row = nmeta[WEST, rows + 2 * (per - 1) + EAST : rows + 2 * (per - 1) + EAST + 1, :]
    lens[at_edge(0, WEST) : at_edge(0, WEST) + 1, :] = jnp.where(has_left, row, 0)

    place = {}
    jcol[...] = jnp.full(jcol.shape, -1, jnp.int32)
    for c in range(per):
        jcol[c * SLOT : (c + 1) * SLOT, :] = meta[c * SLOT : (c + 1) * SLOT, :]
    for i, (c, e) in enumerate(shared):
        place[c, e] = (per + i) * SLOT
        theirs = (0 if e == EAST else per - 1 if e == WEST else c) * SLOT
        jcol[place[c, e] : place[c, e] + SLOT, :] = jnp.where(exists[e], nmeta[e, theirs : theirs + SLOT, :], -1)
    for c in range(per - 1):
        place[c, EAST] = (c + 1) * SLOT
    square = (listed, listed)
    jf = jnp.broadcast_to(jcol[:, 0:1], square).astype(F32)
    jr = jf.T
    row_id = lax.broadcasted_iota(jnp.int32, square, 0)
    lane_id = lax.broadcasted_iota(jnp.int32, square, 1)
    again = jnp.max(jnp.where((jf == jr) & (lane_id < row_id), 1.0, 0.0), axis=1, keepdims=True)
    first = jnp.where(jf[:, 0:1] >= 0.0, 1.0 - again, 0.0)
    first_row = jnp.broadcast_to(first, square).T
    rank = jnp.sum(jnp.where(lane_id < row_id, first_row, 0.0), axis=1, keepdims=True)
    chosen = (jnp.broadcast_to(rank, square) == lane_id.astype(F32)) & (jnp.broadcast_to(first, square) > 0.5)
    u_row = jnp.sum(jnp.where(chosen, jf + 1.0, 0.0), axis=0, keepdims=True) - 1.0
    u_lanes = jnp.broadcast_to(u_row, square)
    u_rows = u_lanes.T
    dmat[...] = jnp.where((u_rows == jr) & (jr >= 0.0), 1.0, 0.0)[0:distinct].astype(BF16)
    dtm[...] = jnp.where((jf == u_lanes) & (jf >= 0.0), 1.0, 0.0).astype(BF16)
    u_block = jnp.broadcast_to(u_row, ub.shape).astype(jnp.int32)
    ub[...] = u_block
    ux[pl.ds(r, 1)] = u_block[None]
    uz[pl.ds(s, 1)] = u_block[None]
    uxc = peers("sx", lambda to: ub, ux.at[r], u_sem.at[0])
    uzc = peers("sy", lambda to: ub, uz.at[s], u_sem.at[1])
    for copy in uxc + uzc:
        copy.start()

    for c in range(1, per):
        ready(c)

    for e in range(4):
        @pl.when(exists[e])
        def _(e=e):
            taken(cnbr.at[pieces(e)[0]], c_recv.at[e])
    for c, e in place:
        if (c, e) in shared:
            theirs = jnp.where(exists[e], cnbr[at_edge(c, e)].astype(F32), 0.0)
        else:
            theirs = cedge[at_edge(c + 1, WEST)].astype(F32)
        both = jnp.concatenate([cedge[at_edge(c, e)].astype(F32), -theirs], axis=0)
        ce[at_edge(c, e)] = both.astype(BF16)

    def setup_response():
        def split(value):
            high = value.astype(BF16)
            return jnp.concatenate([high, (value - high.astype(F32)).astype(BF16)], axis=1)

        rows_in = lax.broadcasted_iota(jnp.int32, (edge, listed), 0)
        for (c, e), at in place.items():
            i = at_edge(c, e)
            corner = jnp.concatenate([dtm[c * SLOT : (c + 1) * SLOT, :], dtm[at : at + SLOT, :]], axis=0)
            share = jnp.dot(ce[i].astype(F32).T.astype(BF16), corner, preferred_element_type=F32)
            inside = rows_in < jnp.broadcast_to(lens[i : i + 1, 0:1], rows_in.shape)
            share = jnp.where(inside, -0.5 * share, 0.0)
            em[c, e * edge : (e + 1) * edge, :] = split(share)
            if is_inner(c, e):
                em[c + 1, WEST * edge : (WEST + 1) * edge, :] = split(-share)
        sol[...] = jnp.zeros(sol.shape, BF16)
        for c in range(per):
            for e in range(4):
                some = slice(e * edge, (e + 1) * edge)
                value = jnp.dot(mats[c, am, some, :], em[c], preferred_element_type=F32)
                gm[c, some, :] = split(value[:, 0:listed] + value[:, listed:])

    def setup_coarse():
        taken(ux.at[0 : nr - 1], u_sem.at[0, 1])
        taken(uz.at[0 : ns - 1], u_sem.at[1, 1])
        k3.wait_recv()
        count = ns * distinct
        wanted = jnp.concatenate(
            [jnp.broadcast_to(uz[q, 0:1, :].astype(F32), square).T[0:distinct, 0:1] for q in range(ns)], axis=0
        )
        at = lax.broadcasted_iota(jnp.int32, (8, nr * tp_rows), 1)
        index = at
        start = [(2 * (m % half) + m // half) * tr for m in range(nr)]
        for m in range(1, nr):
            jump = (start[m] - m * tp_rows) - (start[m - 1] - (m - 1) * tp_rows)
            index = index + jnp.where(at >= m * tp_rows, jump, 0)
        index = index.astype(F32)[0:1]
        lane = lax.broadcasted_iota(jnp.int32, (count, kl), 1)
        picks = [
            jnp.where(
                jnp.broadcast_to(wanted, (count, nr * tp_rows)) == jnp.broadcast_to(index + h * tp_rows, (count, nr * tp_rows)),
                1.0, 0.0,
            ).astype(BF16)
            for h in range(pack)
        ]
        chosen_rows = []
        for q in range(ns):
            plane = kp[:, :, q].astype(F32).reshape(nr * tp_rows, kl).astype(BF16)
            total = jnp.zeros((count, kl), F32)
            for h in range(pack):
                found = jnp.dot(picks[h], plane, preferred_element_type=F32)
                total = jnp.where((lane >= h * tc) & (lane < (h + 1) * tc), found, total)
            chosen_rows.append(total.astype(BF16))
        chosen_rows = jnp.concatenate(chosen_rows, axis=1)
        deep = lax.broadcasted_iota(jnp.int32, (ns * kl, nr * distinct), 0)
        column = jnp.full((ns * kl, nr * distinct), -5, jnp.int32)
        for q in range(ns):
            for h in range(pack):
                low = q * kl + h * tc
                column = jnp.where((deep >= low) & (deep < low + tc), deep - low + q * tc, column)
        listing = jnp.concatenate([ux[q, 0:1, 0:distinct] for q in range(nr)], axis=1)
        pick = jnp.where(column == jnp.broadcast_to(listing, column.shape), 1.0, 0.0).astype(BF16)
        kmat[...] = jnp.dot(chosen_rows, pick, preferred_element_type=F32).astype(BF16)

    def product(mat, c, e):
        return jnp.dot(mats[c, mat, rows_of(e), :], vec[c], preferred_element_type=F32)

    def response(c, e):
        return jnp.dot(gm[c, rows_of(e), :], sol[...], preferred_element_type=F32)

    def keep(k, c, e, sent, value):
        loc[c, rows_of(e)] = value
        if sent:
            snd[k, at_edge(c, e)] = value.astype(BF16)

    def products(k, mat, what, solved):
        for c, e, sent in what:
            value = product(mat, c, e)
            if solved:
                value = value + response(c, e)
            keep(k, c, e, sent, value)

    def started(mat, what):
        for c, e, _ in what:
            loc[c, rows_of(e)] = product(mat, c, e)

    def completed(k, what):
        for c, e, sent in what:
            keep(k, c, e, sent, loc[c, rows_of(e)] + response(c, e))

    def own(c, e):
        return loc[c, rows_of(e)]

    far_edges = [(c, far, True) for c in range(per)]
    near_edges = [(c, near, True) for c in range(per)]
    inner_blocks = [(c, EAST, False) for c in range(per - 1)] + [(c, WEST, False) for c in range(1, per)]

    sides = [(0, WEST, True), (per - 1, EAST, True)]

    place_in_four = lax.rem(r, 4)
    yields = ((place_in_four == 2) & (r + 1 < nr - 1)) | ((place_in_four == 1) & (r > 1))

    def ship_part(k, e, there, low, size):
        here, land = pieces(e)

        @pl.when(there)
        def _():
            pltpu.make_async_remote_copy(
                src_ref=snd.at[k, here, pl.ds(low, size)], dst_ref=rcv.at[k, land, pl.ds(low, size)],
                send_sem=h_send.at[e], recv_sem=h_recv.at[k % 2, opposite(e)],
                device_id=neighbour(e), device_id_type=MESH,
            ).start()

    cut = -(-edge // (2 * SLOT)) * SLOT

    def apply(k, mat, between=None, ready=None):
        solved = ready is not None
        if solved:
            started(mat, far_edges)
            ready()

        def outward():
            if solved:
                completed(k, far_edges)
            else:
                products(k, mat, far_edges, False)
            ship(k, far, has_far)

        def sideways():
            products(k, mat, sides, solved)
            for e in (WEST, EAST):
                ship(k, e, exists[e])

        @pl.when(yields)
        def _():
            sideways()
            outward()

        @pl.when(jnp.logical_not(yields))
        def _():
            outward()
            sideways()

        if between is not None:
            between()
        products(k, mat, near_edges + inner_blocks, solved)
        ship(k, near, has_near)

    def gathered(k, c, e):
        return own(c, e) - rcv[k, at_edge(c, e)].astype(F32)

    def exchanged(k, act):
        for c in range(per - 1):
            act(c, EAST, own(c, EAST) - own(c + 1, WEST))
        arrive(k, near, has_near)
        for c in range(per):
            act(c, near, gathered(k, c, near))
        for c, e in ((0, WEST), (per - 1, EAST)):
            arrive(k, e, exists[e])
            act(c, e, gathered(k, c, e))
        arrive(k, far, has_far)
        for c in range(per):
            act(c, far, gathered(k, c, far))

    def is_inner(c, e):
        return isinstance(e, int) and e == EAST and c < per - 1

    arrive(0, WEST, has_left)
    value = jnp.where(jnp.broadcast_to(has_left, (edge, width)), -rcv[0, at_edge(0, WEST)].astype(F32), 0.0)
    ld[at_edge(0, WEST)] = value
    put(0, WEST, 0.5 * value)
    arrive(0, NORTH, has_up)
    for c in range(per):
        value = jnp.where(jnp.broadcast_to(has_up, (edge, width)), -rcv[0, at_edge(c, NORTH)].astype(F32), 0.0)
        ld[at_edge(c, NORTH)] = value
        put(c, NORTH, 0.5 * value)

    taken(mine.at[0 : ns - 1], k_sem.at[0, 1])
    for copy in k2:
        copy.start()

    halo_round = 1
    ready = None
    for number in range(ITERS):
        apply(halo_round, am, None, ready)

        acc = [jnp.zeros((SLOT, width), F32) for _ in range(listed // SLOT)]
        for (c, e), at in place.items():
            if is_inner(c, e):
                value = own(c, e) - own(c + 1, WEST)
            else:
                value = snd[halo_round, at_edge(c, e)].astype(F32)
            value = jnp.where(mask_of(at_edge(c, e)), value, 0.0).astype(BF16)
            both = jnp.dot(ce[at_edge(c, e)], value, preferred_element_type=F32)
            acc[c] = acc[c] + both[0:SLOT]
            acc[at // SLOT] = acc[at // SLOT] + both[SLOT:]
        terms = 0.5 * jnp.concatenate(acc, axis=0)
        high = terms.astype(BF16)
        low = (terms - high.astype(F32)).astype(BF16)
        terms = jnp.dot(dmat[...], high, preferred_element_type=F32) + jnp.dot(dmat[...], low, preferred_element_type=F32)
        if number > 0:
            terms = terms + momenta[number] * tdir[...]
        tdir[...] = terms
        terms = step_sizes[number] * terms
        if number > 0:
            terms = terms + tsum[...]
        tsum[...] = terms
        terms = terms.astype(BF16)
        ts[number] = terms
        tp[number, pl.ds(r, 1)] = terms[None]
        tcopies = peers("sx", lambda to: ts.at[number], tp.at[number, r], t_sem.at[number])
        for copy in tcopies:
            copy.start()

        if number == 0:
            for c in range(per):
                fetch(c, bm, "wait")
                combine(c, bm)
                if c == 0:
                    taken(kp.at[odd, 0 : half - 1], k_sem.at[1, 1])
                    k3.start()
            setup_coarse()

        def advance(c, e, value):
            i = at_edge(c, e)
            value = jnp.where(mask_of(i), 0.5 * value, 0.0)
            if number == 0:
                iterate = step_sizes[0] * value
            else:
                value = value + momenta[number] * di[i]
                iterate = mu[i] + step_sizes[number] * value
            if number < ITERS - 1:
                di[i] = value
            mu[i] = iterate
            put(c, e, iterate)
            if is_inner(c, e):
                put(c + 1, WEST, -iterate)

        exchanged(halo_round, advance)
        halo_round += 1

        ycopies = peers("sy", lambda to: ys.at[number, to], yr.at[number, s], y_sem.at[number])

        def coarse():
            taken(tp.at[number, 0 : nr - 1], t_sem.at[number, 1])
            partial = jnp.dot(kmat[...], tp[number].reshape(nr * distinct, width), preferred_element_type=F32)
            ys[number] = partial.astype(BF16).reshape(ns, distinct, width)
            yr[number, pl.ds(s, 1)] = ys[number, pl.ds(s, 1)]
            for copy in ycopies:
                copy.start()

        apply(halo_round, bm, coarse)
        if number == ITERS - 1:
            for c in range(per):
                for e in (EAST, SOUTH):
                    mult_out[0, c, e] = mu[at_edge(c, e)]
        if number == 0:
            setup_response()

        def remain(c, e, value):
            i = at_edge(c, e)
            value = 0.5 * (ld[i] - jnp.where(mask_of(i), value, 0.0))
            put(c, e, value)
            if is_inner(c, e):
                put(c + 1, WEST, -value)

        exchanged(halo_round, remain)
        halo_round += 1

        def ready(number=number):
            taken(yr.at[number, 0 : ns - 1], y_sem.at[number, 1])
            solved = yr[number, 0].astype(F32)
            for q in range(1, ns):
                solved = solved + yr[number, q].astype(F32)
            solved = solved.astype(BF16)
            sol[0:distinct] = solved
            sol[listed : listed + distinct] = solved

    norths = [(c, NORTH, True) for c in range(per)]
    started(am, norths)
    ready()
    completed(halo_round, norths)
    ship(halo_round, NORTH, has_up)
    products(halo_round, am, [(0, WEST, True)], True)
    ship(halo_round, WEST, has_left)
    products(
        None, am, [(c, e, False) for c in range(per) for e in (EAST, SOUTH)] + [(c, WEST, False) for c in range(1, per)],
        True,
    )

    def finish(c, e, value):
        prec_out[0, c, e] = jnp.where(mask_of(at_edge(c, e)), 0.5 * value, 0.0)

    for c in range(per - 1):
        finish(c, EAST, own(c, EAST) - own(c + 1, WEST))
    arrive(halo_round, EAST, has_right)
    finish(per - 1, EAST, gathered(halo_round, per - 1, EAST))
    arrive(halo_round, SOUTH, has_down)
    for c in range(per):
        finish(c, SOUTH, gathered(halo_round, c, SOUTH))

    for e in range(4):
        @pl.when(exists[e])
        def _(e=e):
            meta_copy(e).wait_send()
            coupling_copy(e).wait_send()
            taken(snd.at[0:halo_round, pieces(e)[0]], h_send.at[e])
    taken(mine.at[0 : ns - 1], k_sem.at[0, 0])
    taken(kp.at[odd, 0 : half - 1], k_sem.at[1, 0])
    k3.wait_send()
    taken(ux.at[0 : nr - 1], u_sem.at[0, 0])
    taken(uz.at[0 : ns - 1], u_sem.at[1, 0])
    for number in range(ITERS):
        taken(tp.at[number, 0 : nr - 1], t_sem.at[number, 0])
        taken(yr.at[number, 0 : ns - 1], y_sem.at[number, 0])


def hand_over(mult_in, prec_in, mult_out, prec_out, sem):
    copies = [
        pltpu.make_async_copy(mult_in, mult_out, sem.at[0]),
        pltpu.make_async_copy(prec_in, prec_out, sem.at[1]),
    ]
    for copy in copies:
        copy.start()
    for copy in copies:
        copy.wait()


def local(nr, ns, *args):
    adjoint_loads, dual_taut, coupling, coarse_inverse = args[0], args[1], args[5], args[6]
    per, edge, width = adjoint_loads.shape[1], adjoint_loads.shape[3], adjoint_loads.shape[4]
    size = dual_taut.shape[-1]
    corners = coupling.shape[2]
    tr, tc = coarse_inverse.shape
    listed, distinct, pack, tp_rows, kl = sizes_of(nr, ns, per, corners, tr, tc)
    rows = per * SLOT
    rounds = 2 * ITERS + 2
    edges = 4 * per
    meta_rows = rows + -(-2 * per // 8) * 8
    dma = pltpu.SemaphoreType.DMA
    vmem = pl.BlockSpec(memory_space=pltpu.VMEM)
    hbm = pl.BlockSpec(memory_space=pl.ANY)
    args = args[:5] + (jnp.transpose(coupling, (0, 2, 1, 3)),) + args[6:]
    i32 = jnp.int32
    scratch = [
        pltpu.VMEM((per, 4, size, size), BF16),
        pltpu.VMEM((per, size, width), BF16),
        pltpu.VMEM((per, size, width), F32),
        pltpu.VMEM((rounds, edges, edge, width), BF16),
        pltpu.VMEM((rounds, edges, edge, width), BF16),
        pltpu.VMEM((edges, edge, width), F32),
        pltpu.VMEM((edges, edge, width), F32),
        pltpu.VMEM((edges, edge, width), F32),
        pltpu.VMEM(adjoint_loads.shape[1:], F32),
        pltpu.VMEM(args[5].shape[1:], BF16),
        pltpu.VMEM((tr, tc), BF16),
        pltpu.SMEM(args[7].shape, i32),
        pltpu.SMEM(args[8].shape, i32),
        pltpu.SMEM(args[9].shape, i32),
        pltpu.VMEM((meta_rows, LANES), i32),
        pltpu.VMEM((4, meta_rows, LANES), i32),
        pltpu.VMEM((-(-edges // 8) * 8, LANES), i32),
        pltpu.VMEM((listed, LANES), i32),
        pltpu.VMEM((distinct, listed), BF16),
        pltpu.VMEM((listed, listed), BF16),
        pltpu.VMEM((8, listed), i32),
        pltpu.VMEM((nr, 8, listed), i32),
        pltpu.VMEM((ns, 8, listed), i32),
        pltpu.VMEM((2, nr // 2, ns, tp_rows, kl), BF16),
        pltpu.VMEM((ns * distinct, nr * distinct), BF16),
        pltpu.VMEM((edges, SLOT, edge), BF16),
        pltpu.VMEM((edges, SLOT, edge), BF16),
        pltpu.VMEM((edges, 2 * SLOT, edge), BF16),
        pltpu.VMEM((per, size, 2 * listed), BF16),
        pltpu.VMEM((per, size, 2 * listed), BF16),
        pltpu.VMEM((2 * listed, width), BF16),
        pltpu.VMEM((distinct, width), F32),
        pltpu.VMEM((distinct, width), F32),
        pltpu.VMEM((ITERS, distinct, width), BF16),
        pltpu.VMEM((ITERS, nr, distinct, width), BF16),
        pltpu.VMEM((ITERS, ns, distinct, width), BF16),
        pltpu.VMEM((ITERS, ns, distinct, width), BF16),
        dma((per,)), dma((6,)),
        dma((4,)), dma((2, 4)),
        dma((4,)), dma((4,)),
        dma((4,)), dma((4,)),
        dma((2, 2)), dma((3, 2)), dma((ITERS, 2)), dma((ITERS, 2)),
    ]
    out = jax.ShapeDtypeStruct(adjoint_loads.shape, F32)
    kept = pltpu.VMEM(adjoint_loads.shape, F32)
    results = pl.pallas_call(
        functools.partial(kernel, nr, ns),
        out_shape=(kept, kept),
        in_specs=[hbm] * 10,
        out_specs=(vmem, vmem),
        scratch_shapes=scratch,
        compiler_params=pltpu.CompilerParams(
            collective_id=0, has_side_effects=True, vmem_limit_bytes=56 * 1024 * 1024
        ),
    )(*args)
    results = [pltpu.with_memory_space_constraint(x, pltpu.VMEM) for x in results]
    return pl.pallas_call(
        hand_over, out_shape=(out, out), in_specs=[vmem, vmem], out_specs=(hbm, hbm), scratch_shapes=[dma((2,))],
    )(*results)


def solution(mesh):
    placed = (
        P("sx", "sy", None, None, None),
        P("sx", "sy", None, None),
        P("sx", "sy", None, None),
        P("sx", "sy", None, None),
        P("sx", "sy", None, None),
        P("sx", "sy", None, None),
        P("sx", "sy"),
        P("sx", "sy"),
        P("sx", "sy", None),
        P("sx", "sy", None),
    )
    return jax.shard_map(
        functools.partial(local, mesh.shape["sx"], mesh.shape["sy"]),
        mesh=mesh,
        in_specs=placed,
        out_specs=(P("sx", "sy", None, None, None), P("sx", "sy", None, None, None)),
        check_vma=False,
    )
```

```python
import functools

import jax
import jax.numpy as jnp
from jax import lax
from jax.experimental import pallas as pl
from jax.experimental.pallas import tpu as pltpu
from jax.sharding import PartitionSpec as P

ITERS = 2
step_sizes = (0.55, 0.75)
momenta = (0.0, 0.15)

MESH = pl.DeviceIdType.MESH
SLOT = 16
LANES = 128
F32 = jnp.float32
BF16 = jnp.bfloat16
EAST, SOUTH, WEST, NORTH = 0, 1, 2, 3


def sizes_of(nr, ns, per, corners, tr, tc):
    listed = -(-(3 * per + 2) * SLOT // LANES) * LANES
    distinct = -(-(corners // 4) * (4 * per + 8) // SLOT) * SLOT
    pack = 2 if 2 * tc <= LANES and tr % (2 * SLOT) == 0 else 1
    lanes = -(-pack * tc // LANES) * LANES
    return listed, distinct, pack, tr // pack, lanes


def kernel(
    nr, ns,
    loads_in, dual_t, dual_w, diri_t, diri_w, coup_in, cinv_in, wr_in, len_in, cm_in,
    mult_out, prec_out,
    mats, vec, loc, snd, rcv, ld, mu, di,
    lraw, craw, vraw, wr_ref, len_ref, cm_ref,
    meta, nmeta, lens, jcol, dmat, dtm, ub, ux, uz, kp, kmat,
    cedge, cnbr, ce, em, gm, sol, tdir, tsum, ts, tp, ys, yr,
    mat_sem, in_sem, h_send, h_recv, m_send, m_recv, c_send, c_recv, u_sem, k_sem, t_sem, y_sem,
):
    r, s = lax.axis_index("sx"), lax.axis_index("sy")
    per = loads_in.shape[1]
    edge, width = loads_in.shape[3], loads_in.shape[4]
    corners = coup_in.shape[1]
    tr, tc = cinv_in.shape
    listed, distinct, pack, tp_rows, kl = sizes_of(nr, ns, per, corners, tr, tc)
    rows = per * SLOT
    half = nr // 2
    odd = lax.rem(r, 2)
    has_left, has_right = s > 0, s < ns - 1
    has_up, has_down = r > 0, r < nr - 1
    exists = {EAST: has_right, SOUTH: has_down, WEST: has_left, NORTH: has_up}
    far, near = 3 - 2 * odd, 1 + 2 * odd
    has_far = ((odd == 1) & has_down) | ((odd == 0) & has_up)
    has_near = None if nr % 2 == 0 else ((odd == 0) & has_down) | ((odd == 1) & has_up)

    barrier = pltpu.get_barrier_semaphore()
    for k in range(1, nr):
        pl.semaphore_signal(barrier, inc=1, device_id={"sx": lax.rem(r + k, nr)}, device_id_type=MESH)
    for k in range(1, ns):
        pl.semaphore_signal(barrier, inc=1, device_id={"sy": lax.rem(s + k, ns)}, device_id_type=MESH)

    small = [
        pltpu.make_async_copy(src, dst, in_sem.at[i])
        for i, (src, dst) in enumerate(
            ((wr_in, wr_ref), (len_in, len_ref), (cm_in, cm_ref), (loads_in.at[0], lraw), (coup_in.at[0], craw), (cinv_in, vraw))
        )
    ]
    for copy in small:
        copy.start()
    am, aw, bm, bw = 0, 1, 2, 3

    def fetch(c, first, act):
        if act == "start":
            for i, src in enumerate((diri_t, diri_w) if first == am else (dual_t, dual_w)):
                pltpu.make_async_copy(src.at[0, c], mats.at[c, first + i], mat_sem.at[c]).start()
        else:
            both = mats.at[c, first : first + 2]
            pltpu.make_async_copy(both, both, mat_sem.at[c]).wait()

    positions = lax.broadcasted_iota(jnp.int32, (edge, width), 0)

    def live(row):
        return positions < jnp.broadcast_to(row, (edge, width))

    def mask_of(i):
        return live(lens[pl.ds(i, 1), :])

    def at_edge(c, e):
        return e * per + c

    def rows_of(e):
        return pl.ds(pl.multiple_of(e * edge, SLOT), edge)

    def put(c, e, value):
        vec[c, rows_of(e)] = value.astype(BF16)

    def pieces(e):
        if isinstance(e, int) and e in (EAST, WEST):
            here, there = (per - 1, 0) if e == EAST else (0, per - 1)
            return pl.ds(e * per + here, 1), pl.ds((2 - e) * per + there, 1)
        return pl.ds(e * per, per), pl.ds((4 - e) * per, per)

    def neighbour(e):
        return {"sy": s + (1 - e)} if isinstance(e, int) and e in (EAST, WEST) else {"sx": r + (2 - e)}

    def opposite(e):
        return 2 - e if isinstance(e, int) and e in (EAST, WEST) else 4 - e

    def xfer(k, e):
        here, there = pieces(e)
        return pltpu.make_async_remote_copy(
            src_ref=snd.at[k, here], dst_ref=rcv.at[k, there], send_sem=h_send.at[e], recv_sem=h_recv.at[k % 2, opposite(e)],
            device_id=neighbour(e), device_id_type=MESH,
        )

    def ship(k, e, there):
        here, land = pieces(e)
        size = edge // 1

        def go():
            for c in range(here.size):
                for i in range(1):
                    some = pl.ds(i * size, size)
                    pltpu.make_async_remote_copy(
                        src_ref=snd.at[k, here.start + c, some], dst_ref=rcv.at[k, land.start + c, some],
                        send_sem=h_send.at[e], recv_sem=h_recv.at[k % 2, opposite(e)],
                        device_id=neighbour(e), device_id_type=MESH,
                    ).start()

        if there is None:
            go()
        else:
            pl.when(there)(go)

    def taken(ref, sem):
        pltpu.make_async_copy(ref, ref, sem).wait()

    def arrive(k, e, there):
        if there is None:
            taken(rcv.at[k, pieces(e)[0]], h_recv.at[k % 2, e])
        else:
            pl.when(there)(lambda: taken(rcv.at[k, pieces(e)[0]], h_recv.at[k % 2, e]))

    def peers(axis, src, dst, sems):
        n, me = (nr, r) if axis == "sx" else (ns, s)
        out = []
        for k in range(1, n):
            to = lax.rem(me + jnp.where(me < n // 2, n - k, k), n)
            out.append(
                pltpu.make_async_remote_copy(
                    src_ref=src(to), dst_ref=dst, send_sem=sems.at[0], recv_sem=sems.at[1],
                    device_id={axis: to}, device_id_type=MESH,
                )
            )
        return out

    def meta_copy(e):
        return pltpu.make_async_remote_copy(
            src_ref=meta, dst_ref=nmeta.at[opposite(e)], send_sem=m_send.at[e], recv_sem=m_recv.at[opposite(e)],
            device_id=neighbour(e), device_id_type=MESH,
        )

    def coupling_copy(e):
        here, there = pieces(e)
        return pltpu.make_async_remote_copy(
            src_ref=cedge.at[here], dst_ref=cnbr.at[there], send_sem=c_send.at[e], recv_sem=c_recv.at[opposite(e)],
            device_id=neighbour(e), device_id_type=MESH,
        )

    shared = [(c, SOUTH) for c in range(per)] + [(c, NORTH) for c in range(per)] + [(per - 1, EAST), (0, WEST)]

    for copy in small[:3]:
        copy.wait()
    for c in range(per):
        fetch(c, am, "start")
    meta[...] = jnp.full(meta.shape, -1, jnp.int32)
    for c in range(per):
        for m in range(corners):
            meta[c * SLOT + m : c * SLOT + m + 1, :] = jnp.full((1, LANES), cm_ref[0, c, m], jnp.int32)
        east = len_ref[0, c, 0]
        if c == per - 1:
            east = jnp.where(has_right, east, 0)
        south = jnp.where(has_down, len_ref[0, c, 1], 0)
        for e, length in ((EAST, east), (SOUTH, south)):
            row = jnp.full((1, LANES), length, jnp.int32)
            meta[rows + 2 * c + e : rows + 2 * c + e + 1, :] = row
            lens[at_edge(c, e) : at_edge(c, e) + 1, :] = row
    small[3].wait()
    for c in range(per):
        for e in (EAST, SOUTH):
            value = jnp.where(live(lens[at_edge(c, e) : at_edge(c, e) + 1, :]), lraw[c, e], 0.0)
            ld[at_edge(c, e)] = value
            put(c, e, 0.5 * value)
            if e == SOUTH or c == per - 1:
                snd[0, at_edge(c, e)] = value.astype(BF16)
            else:
                put(c + 1, WEST, -0.5 * value)

    small[5].wait()
    tile = vraw[...].astype(F32)
    parts = [tile[h * tp_rows : (h + 1) * tp_rows] for h in range(pack)]
    if kl > pack * tc:
        parts.append(jnp.zeros((tp_rows, kl - pack * tc), F32))
    kp[odd, lax.div(r, 2), s] = jnp.concatenate(parts, axis=1).astype(BF16)
    mine = kp.at[odd, lax.div(r, 2)]
    k1 = peers("sy", lambda to: mine.at[s], mine.at[s], k_sem.at[0])
    k2 = [
        pltpu.make_async_remote_copy(
            src_ref=mine, dst_ref=mine, send_sem=k_sem.at[1, 0], recv_sem=k_sem.at[1, 1],
            device_id={"sx": lax.rem(r + 2 * k, nr)}, device_id_type=MESH,
        )
        for k in range(1, half)
    ]
    k3 = pltpu.make_async_remote_copy(
        src_ref=kp.at[odd], dst_ref=kp.at[odd], send_sem=k_sem.at[2, 0], recv_sem=k_sem.at[2, 1],
        device_id={"sx": r + 1 - 2 * odd}, device_id_type=MESH,
    )
    pl.semaphore_wait(barrier, nr - 1 + ns - 1)
    for e in range(4):
        @pl.when(exists[e])
        def _(e=e):
            meta_copy(e).start()
    for copy in k1:
        copy.start()
    ship(0, SOUTH, has_down)
    ship(0, EAST, has_right)
    small[4].wait()
    for c in range(per):
        whole = jnp.concatenate(
            [craw[:, c, :].astype(F32), jnp.zeros((SLOT - corners, craw.shape[2]), F32)], axis=0
        )
        turned = whole.T
        for e in range(4):
            cedge[at_edge(c, e)] = turned[e * edge : (e + 1) * edge].T.astype(BF16)
    for e in range(4):
        @pl.when(exists[e])
        def _(e=e):
            coupling_copy(e).start()

    def combine(c, main):
        flag = jnp.full((1, 1), wr_ref[0, c], jnp.int32).astype(F32).astype(BF16)
        size = mats.shape[2]
        step = 128

        def body(i, _):
            part = pl.ds(pl.multiple_of(i * step, step), step)
            mats[c, main, part] = mats[c, main, part] + flag * mats[c, main + 1, part]
            return 0

        lax.fori_loop(0, size // step, body, 0)

    def ready(c):
        fetch(c, am, "wait")
        fetch(c, bm, "start")
        combine(c, am)

    ready(0)

    for e in range(4):
        @pl.when(exists[e])
        def _(e=e):
            taken(nmeta.at[e], m_recv.at[e])
    for c in range(per):
        row = nmeta[NORTH, rows + 2 * c + SOUTH : rows + 2 * c + SOUTH + 1, :]
        lens[at_edge(c, NORTH) : at_edge(c, NORTH) + 1, :] = jnp.where(has_up, row, 0)
    row = nmeta[WEST, rows + 2 * (per - 1) + EAST : rows + 2 * (per - 1) + EAST + 1, :]
    lens[at_edge(0, WEST) : at_edge(0, WEST) + 1, :] = jnp.where(has_left, row, 0)

    place = {}
    jcol[...] = jnp.full(jcol.shape, -1, jnp.int32)
    for c in range(per):
        jcol[c * SLOT : (c + 1) * SLOT, :] = meta[c * SLOT : (c + 1) * SLOT, :]
    for i, (c, e) in enumerate(shared):
        place[c, e] = (per + i) * SLOT
        theirs = (0 if e == EAST else per - 1 if e == WEST else c) * SLOT
        jcol[place[c, e] : place[c, e] + SLOT, :] = jnp.where(exists[e], nmeta[e, theirs : theirs + SLOT, :], -1)
    for c in range(per - 1):
        place[c, EAST] = (c + 1) * SLOT
    square = (listed, listed)
    jf = jnp.broadcast_to(jcol[:, 0:1], square).astype(F32)
    jr = jf.T
    row_id = lax.broadcasted_iota(jnp.int32, square, 0)
    lane_id = lax.broadcasted_iota(jnp.int32, square, 1)
    again = jnp.max(jnp.where((jf == jr) & (lane_id < row_id), 1.0, 0.0), axis=1, keepdims=True)
    first = jnp.where(jf[:, 0:1] >= 0.0, 1.0 - again, 0.0)
    first_row = jnp.broadcast_to(first, square).T
    rank = jnp.sum(jnp.where(lane_id < row_id, first_row, 0.0), axis=1, keepdims=True)
    chosen = (jnp.broadcast_to(rank, square) == lane_id.astype(F32)) & (jnp.broadcast_to(first, square) > 0.5)
    u_row = jnp.sum(jnp.where(chosen, jf + 1.0, 0.0), axis=0, keepdims=True) - 1.0
    u_lanes = jnp.broadcast_to(u_row, square)
    u_rows = u_lanes.T
    dmat[...] = jnp.where((u_rows == jr) & (jr >= 0.0), 1.0, 0.0)[0:distinct].astype(BF16)
    dtm[...] = jnp.where((jf == u_lanes) & (jf >= 0.0), 1.0, 0.0).astype(BF16)
    u_block = jnp.broadcast_to(u_row, ub.shape).astype(jnp.int32)
    ub[...] = u_block
    ux[pl.ds(r, 1)] = u_block[None]
    uz[pl.ds(s, 1)] = u_block[None]
    uxc = peers("sx", lambda to: ub, ux.at[r], u_sem.at[0])
    uzc = peers("sy", lambda to: ub, uz.at[s], u_sem.at[1])
    for copy in uxc + uzc:
        copy.start()

    for c in range(1, per):
        ready(c)

    for e in range(4):
        @pl.when(exists[e])
        def _(e=e):
            taken(cnbr.at[pieces(e)[0]], c_recv.at[e])
    for c, e in place:
        if (c, e) in shared:
            theirs = jnp.where(exists[e], cnbr[at_edge(c, e)].astype(F32), 0.0)
        else:
            theirs = cedge[at_edge(c + 1, WEST)].astype(F32)
        both = jnp.concatenate([cedge[at_edge(c, e)].astype(F32), -theirs], axis=0)
        ce[at_edge(c, e)] = both.astype(BF16)

    def setup_response():
        def split(value):
            high = value.astype(BF16)
            return jnp.concatenate([high, (value - high.astype(F32)).astype(BF16)], axis=1)

        rows_in = lax.broadcasted_iota(jnp.int32, (edge, listed), 0)
        for (c, e), at in place.items():
            i = at_edge(c, e)
            corner = jnp.concatenate([dtm[c * SLOT : (c + 1) * SLOT, :], dtm[at : at + SLOT, :]], axis=0)
            share = jnp.dot(ce[i].astype(F32).T.astype(BF16), corner, preferred_element_type=F32)
            inside = rows_in < jnp.broadcast_to(lens[i : i + 1, 0:1], rows_in.shape)
            share = jnp.where(inside, -0.5 * share, 0.0)
            em[c, e * edge : (e + 1) * edge, :] = split(share)
            if is_inner(c, e):
                em[c + 1, WEST * edge : (WEST + 1) * edge, :] = split(-share)
        sol[...] = jnp.zeros(sol.shape, BF16)
        for c in range(per):
            for e in range(4):
                some = slice(e * edge, (e + 1) * edge)
                value = jnp.dot(mats[c, am, some, :], em[c], preferred_element_type=F32)
                gm[c, some, :] = split(value[:, 0:listed] + value[:, listed:])

    def setup_coarse():
        taken(ux.at[0 : nr - 1], u_sem.at[0, 1])
        taken(uz.at[0 : ns - 1], u_sem.at[1, 1])
        k3.wait_recv()
        count = ns * distinct
        wanted = jnp.concatenate(
            [jnp.broadcast_to(uz[q, 0:1, :].astype(F32), square).T[0:distinct, 0:1] for q in range(ns)], axis=0
        )
        at = lax.broadcasted_iota(jnp.int32, (8, nr * tp_rows), 1)
        index = at
        start = [(2 * (m % half) + m // half) * tr for m in range(nr)]
        for m in range(1, nr):
            jump = (start[m] - m * tp_rows) - (start[m - 1] - (m - 1) * tp_rows)
            index = index + jnp.where(at >= m * tp_rows, jump, 0)
        index = index.astype(F32)[0:1]
        lane = lax.broadcasted_iota(jnp.int32, (count, kl), 1)
        picks = [
            jnp.where(
                jnp.broadcast_to(wanted, (count, nr * tp_rows)) == jnp.broadcast_to(index + h * tp_rows, (count, nr * tp_rows)),
                1.0, 0.0,
            ).astype(BF16)
            for h in range(pack)
        ]
        chosen_rows = []
        for q in range(ns):
            plane = kp[:, :, q].astype(F32).reshape(nr * tp_rows, kl).astype(BF16)
            total = jnp.zeros((count, kl), F32)
            for h in range(pack):
                found = jnp.dot(picks[h], plane, preferred_element_type=F32)
                total = jnp.where((lane >= h * tc) & (lane < (h + 1) * tc), found, total)
            chosen_rows.append(total.astype(BF16))
        chosen_rows = jnp.concatenate(chosen_rows, axis=1)
        deep = lax.broadcasted_iota(jnp.int32, (ns * kl, nr * distinct), 0)
        column = jnp.full((ns * kl, nr * distinct), -5, jnp.int32)
        for q in range(ns):
            for h in range(pack):
                low = q * kl + h * tc
                column = jnp.where((deep >= low) & (deep < low + tc), deep - low + q * tc, column)
        listing = jnp.concatenate([ux[q, 0:1, 0:distinct] for q in range(nr)], axis=1)
        pick = jnp.where(column == jnp.broadcast_to(listing, column.shape), 1.0, 0.0).astype(BF16)
        kmat[...] = jnp.dot(chosen_rows, pick, preferred_element_type=F32).astype(BF16)

    def product(mat, c, e):
        return jnp.dot(mats[c, mat, rows_of(e), :], vec[c], preferred_element_type=F32)

    def response(c, e):
        return jnp.dot(gm[c, rows_of(e), :], sol[...], preferred_element_type=F32)

    def keep(k, c, e, sent, value):
        loc[c, rows_of(e)] = value
        if sent:
            snd[k, at_edge(c, e)] = value.astype(BF16)

    def products(k, mat, what, solved):
        for c, e, sent in what:
            value = product(mat, c, e)
            if solved:
                value = value + response(c, e)
            keep(k, c, e, sent, value)

    def started(mat, what):
        for c, e, _ in what:
            loc[c, rows_of(e)] = product(mat, c, e)

    def completed(k, what):
        for c, e, sent in what:
            keep(k, c, e, sent, loc[c, rows_of(e)] + response(c, e))

    def own(c, e):
        return loc[c, rows_of(e)]

    far_edges = [(c, far, True) for c in range(per)]
    near_edges = [(c, near, True) for c in range(per)]
    inner_blocks = [(c, EAST, False) for c in range(per - 1)] + [(c, WEST, False) for c in range(1, per)]

    sides = [(0, WEST, True), (per - 1, EAST, True)]

    place_in_four = lax.rem(r, 4)
    yields = ((place_in_four == 2) & (r + 1 < nr - 1)) | ((place_in_four == 1) & (r > 1))

    def ship_part(k, e, there, low, size):
        here, land = pieces(e)

        @pl.when(there)
        def _():
            pltpu.make_async_remote_copy(
                src_ref=snd.at[k, here, pl.ds(low, size)], dst_ref=rcv.at[k, land, pl.ds(low, size)],
                send_sem=h_send.at[e], recv_sem=h_recv.at[k % 2, opposite(e)],
                device_id=neighbour(e), device_id_type=MESH,
            ).start()

    cut = -(-edge // (2 * SLOT)) * SLOT

    def apply(k, mat, between=None, ready=None):
        solved = ready is not None
        if solved:
            started(mat, far_edges)
            ready()

        def outward():
            if solved:
                completed(k, far_edges)
            else:
                products(k, mat, far_edges, False)
            ship(k, far, has_far)

        def sideways():
            products(k, mat, sides, solved)
            for e in (WEST, EAST):
                ship(k, e, exists[e])

        @pl.when(yields)
        def _():
            sideways()
            outward()

        @pl.when(jnp.logical_not(yields))
        def _():
            outward()
            sideways()

        if between is not None:
            between()
        products(k, mat, near_edges + inner_blocks, solved)
        ship(k, near, has_near)

    def gathered(k, c, e):
        return own(c, e) - rcv[k, at_edge(c, e)].astype(F32)

    def exchanged(k, act):
        for c in range(per - 1):
            act(c, EAST, own(c, EAST) - own(c + 1, WEST))
        arrive(k, near, has_near)
        for c in range(per):
            act(c, near, gathered(k, c, near))
        for c, e in ((0, WEST), (per - 1, EAST)):
            arrive(k, e, exists[e])
            act(c, e, gathered(k, c, e))
        arrive(k, far, has_far)
        for c in range(per):
            act(c, far, gathered(k, c, far))

    def is_inner(c, e):
        return isinstance(e, int) and e == EAST and c < per - 1

    arrive(0, WEST, has_left)
    value = jnp.where(jnp.broadcast_to(has_left, (edge, width)), -rcv[0, at_edge(0, WEST)].astype(F32), 0.0)
    ld[at_edge(0, WEST)] = value
    put(0, WEST, 0.5 * value)
    arrive(0, NORTH, has_up)
    for c in range(per):
        value = jnp.where(jnp.broadcast_to(has_up, (edge, width)), -rcv[0, at_edge(c, NORTH)].astype(F32), 0.0)
        ld[at_edge(c, NORTH)] = value
        put(c, NORTH, 0.5 * value)

    taken(mine.at[0 : ns - 1], k_sem.at[0, 1])
    for copy in k2:
        copy.start()

    halo_round = 1
    ready = None
    for number in range(ITERS):
        apply(halo_round, am, None, ready)

        acc = [jnp.zeros((SLOT, width), F32) for _ in range(listed // SLOT)]
        for (c, e), at in place.items():
            if is_inner(c, e):
                value = own(c, e) - own(c + 1, WEST)
            else:
                value = snd[halo_round, at_edge(c, e)].astype(F32)
            value = jnp.where(mask_of(at_edge(c, e)), value, 0.0).astype(BF16)
            both = jnp.dot(ce[at_edge(c, e)], value, preferred_element_type=F32)
            acc[c] = acc[c] + both[0:SLOT]
            acc[at // SLOT] = acc[at // SLOT] + both[SLOT:]
        terms = 0.5 * jnp.concatenate(acc, axis=0)
        high = terms.astype(BF16)
        low = (terms - high.astype(F32)).astype(BF16)
        terms = jnp.dot(dmat[...], high, preferred_element_type=F32) + jnp.dot(dmat[...], low, preferred_element_type=F32)
        if number > 0:
            terms = terms + momenta[number] * tdir[...]
        tdir[...] = terms
        terms = step_sizes[number] * terms
        if number > 0:
            terms = terms + tsum[...]
        tsum[...] = terms
        terms = terms.astype(BF16)
        ts[number] = terms
        tp[number, pl.ds(r, 1)] = terms[None]
        tcopies = peers("sx", lambda to: ts.at[number], tp.at[number, r], t_sem.at[number])
        for copy in tcopies:
            copy.start()

        if number == 0:
            for c in range(per):
                fetch(c, bm, "wait")
                combine(c, bm)
                if c == 0:
                    taken(kp.at[odd, 0 : half - 1], k_sem.at[1, 1])
                    k3.start()
            setup_coarse()

        def advance(c, e, value):
            i = at_edge(c, e)
            value = jnp.where(mask_of(i), 0.5 * value, 0.0)
            if number == 0:
                iterate = step_sizes[0] * value
            else:
                value = value + momenta[number] * di[i]
                iterate = mu[i] + step_sizes[number] * value
            if number < ITERS - 1:
                di[i] = value
            mu[i] = iterate
            put(c, e, iterate)
            if is_inner(c, e):
                put(c + 1, WEST, -iterate)

        exchanged(halo_round, advance)
        halo_round += 1

        ycopies = peers("sy", lambda to: ys.at[number, to], yr.at[number, s], y_sem.at[number])

        def coarse():
            taken(tp.at[number, 0 : nr - 1], t_sem.at[number, 1])
            partial = jnp.dot(kmat[...], tp[number].reshape(nr * distinct, width), preferred_element_type=F32)
            ys[number] = partial.astype(BF16).reshape(ns, distinct, width)
            yr[number, pl.ds(s, 1)] = ys[number, pl.ds(s, 1)]
            for copy in ycopies:
                copy.start()

        apply(halo_round, bm, coarse)
        if number == ITERS - 1:
            for c in range(per):
                for e in (EAST, SOUTH):
                    mult_out[0, c, e] = mu[at_edge(c, e)]
        if number == 0:
            setup_response()

        def remain(c, e, value):
            i = at_edge(c, e)
            value = 0.5 * (ld[i] - jnp.where(mask_of(i), value, 0.0))
            put(c, e, value)
            if is_inner(c, e):
                put(c + 1, WEST, -value)

        exchanged(halo_round, remain)
        halo_round += 1

        def ready(number=number):
            taken(yr.at[number, 0 : ns - 1], y_sem.at[number, 1])
            solved = yr[number, 0].astype(F32)
            for q in range(1, ns):
                solved = solved + yr[number, q].astype(F32)
            solved = solved.astype(BF16)
            sol[0:distinct] = solved
            sol[listed : listed + distinct] = solved

    norths = [(c, NORTH, True) for c in range(per)]
    started(am, norths)
    ready()
    completed(halo_round, norths)
    ship(halo_round, NORTH, has_up)
    products(halo_round, am, [(0, WEST, True)], True)
    ship(halo_round, WEST, has_left)
    products(
        None, am, [(c, e, False) for c in range(per) for e in (EAST, SOUTH)] + [(c, WEST, False) for c in range(1, per)],
        True,
    )

    def finish(c, e, value):
        prec_out[0, c, e] = jnp.where(mask_of(at_edge(c, e)), 0.5 * value, 0.0)

    for c in range(per - 1):
        finish(c, EAST, own(c, EAST) - own(c + 1, WEST))
    arrive(halo_round, EAST, has_right)
    finish(per - 1, EAST, gathered(halo_round, per - 1, EAST))
    arrive(halo_round, SOUTH, has_down)
    for c in range(per):
        finish(c, SOUTH, gathered(halo_round, c, SOUTH))

    for e in range(4):
        @pl.when(exists[e])
        def _(e=e):
            meta_copy(e).wait_send()
            coupling_copy(e).wait_send()
            taken(snd.at[0:halo_round, pieces(e)[0]], h_send.at[e])
    taken(mine.at[0 : ns - 1], k_sem.at[0, 0])
    taken(kp.at[odd, 0 : half - 1], k_sem.at[1, 0])
    k3.wait_send()
    taken(ux.at[0 : nr - 1], u_sem.at[0, 0])
    taken(uz.at[0 : ns - 1], u_sem.at[1, 0])
    for number in range(ITERS):
        taken(tp.at[number, 0 : nr - 1], t_sem.at[number, 0])
        taken(yr.at[number, 0 : ns - 1], y_sem.at[number, 0])


def hand_over(mult_in, prec_in, mult_out, prec_out, sem):
    copies = [
        pltpu.make_async_copy(src.at[0, c, e], dst.at[0, c, e], sem.at[i, c, e])
        for i, (src, dst) in enumerate(((mult_in, mult_out), (prec_in, prec_out)))
        for c in range(mult_in.shape[1])
        for e in range(2)
    ]
    for copy in copies:
        copy.start()
    for copy in copies:
        copy.wait()


def local(nr, ns, *args):
    adjoint_loads, dual_taut, coupling, coarse_inverse = args[0], args[1], args[5], args[6]
    per, edge, width = adjoint_loads.shape[1], adjoint_loads.shape[3], adjoint_loads.shape[4]
    size = dual_taut.shape[-1]
    corners = coupling.shape[2]
    tr, tc = coarse_inverse.shape
    listed, distinct, pack, tp_rows, kl = sizes_of(nr, ns, per, corners, tr, tc)
    rows = per * SLOT
    rounds = 2 * ITERS + 2
    edges = 4 * per
    meta_rows = rows + -(-2 * per // 8) * 8
    dma = pltpu.SemaphoreType.DMA
    vmem = pl.BlockSpec(memory_space=pltpu.VMEM)
    hbm = pl.BlockSpec(memory_space=pl.ANY)
    args = args[:5] + (jnp.transpose(coupling, (0, 2, 1, 3)),) + args[6:]
    i32 = jnp.int32
    scratch = [
        pltpu.VMEM((per, 4, size, size), BF16),
        pltpu.VMEM((per, size, width), BF16),
        pltpu.VMEM((per, size, width), F32),
        pltpu.VMEM((rounds, edges, edge, width), BF16),
        pltpu.VMEM((rounds, edges, edge, width), BF16),
        pltpu.VMEM((edges, edge, width), F32),
        pltpu.VMEM((edges, edge, width), F32),
        pltpu.VMEM((edges, edge, width), F32),
        pltpu.VMEM(adjoint_loads.shape[1:], F32),
        pltpu.VMEM(args[5].shape[1:], BF16),
        pltpu.VMEM((tr, tc), BF16),
        pltpu.SMEM(args[7].shape, i32),
        pltpu.SMEM(args[8].shape, i32),
        pltpu.SMEM(args[9].shape, i32),
        pltpu.VMEM((meta_rows, LANES), i32),
        pltpu.VMEM((4, meta_rows, LANES), i32),
        pltpu.VMEM((-(-edges // 8) * 8, LANES), i32),
        pltpu.VMEM((listed, LANES), i32),
        pltpu.VMEM((distinct, listed), BF16),
        pltpu.VMEM((listed, listed), BF16),
        pltpu.VMEM((8, listed), i32),
        pltpu.VMEM((nr, 8, listed), i32),
        pltpu.VMEM((ns, 8, listed), i32),
        pltpu.VMEM((2, nr // 2, ns, tp_rows, kl), BF16),
        pltpu.VMEM((ns * distinct, nr * distinct), BF16),
        pltpu.VMEM((edges, SLOT, edge), BF16),
        pltpu.VMEM((edges, SLOT, edge), BF16),
        pltpu.VMEM((edges, 2 * SLOT, edge), BF16),
        pltpu.VMEM((per, size, 2 * listed), BF16),
        pltpu.VMEM((per, size, 2 * listed), BF16),
        pltpu.VMEM((2 * listed, width), BF16),
        pltpu.VMEM((distinct, width), F32),
        pltpu.VMEM((distinct, width), F32),
        pltpu.VMEM((ITERS, distinct, width), BF16),
        pltpu.VMEM((ITERS, nr, distinct, width), BF16),
        pltpu.VMEM((ITERS, ns, distinct, width), BF16),
        pltpu.VMEM((ITERS, ns, distinct, width), BF16),
        dma((per,)), dma((6,)),
        dma((4,)), dma((2, 4)),
        dma((4,)), dma((4,)),
        dma((4,)), dma((4,)),
        dma((2, 2)), dma((3, 2)), dma((ITERS, 2)), dma((ITERS, 2)),
    ]
    out = jax.ShapeDtypeStruct(adjoint_loads.shape, F32)
    kept = pltpu.VMEM(adjoint_loads.shape, F32)
    results = pl.pallas_call(
        functools.partial(kernel, nr, ns),
        out_shape=(kept, kept),
        in_specs=[hbm] * 10,
        out_specs=(vmem, vmem),
        scratch_shapes=scratch,
        compiler_params=pltpu.CompilerParams(
            collective_id=0, has_side_effects=True, vmem_limit_bytes=56 * 1024 * 1024
        ),
    )(*args)
    results = [pltpu.with_memory_space_constraint(x, pltpu.VMEM) for x in results]
    return pl.pallas_call(
        hand_over, out_shape=(out, out), in_specs=[vmem, vmem], out_specs=(hbm, hbm), scratch_shapes=[dma((2, per, 2))],
    )(*results)


def solution(mesh):
    placed = (
        P("sx", "sy", None, None, None),
        P("sx", "sy", None, None),
        P("sx", "sy", None, None),
        P("sx", "sy", None, None),
        P("sx", "sy", None, None),
        P("sx", "sy", None, None),
        P("sx", "sy"),
        P("sx", "sy"),
        P("sx", "sy", None),
        P("sx", "sy", None),
    )
    return jax.shard_map(
        functools.partial(local, mesh.shape["sx"], mesh.shape["sy"]),
        mesh=mesh,
        in_specs=placed,
        out_specs=(P("sx", "sy", None, None, None), P("sx", "sy", None, None, None)),
        check_vma=False,
    )
```
